768 devices in a mesh: seq: 12 (over z), head: 64 (over y, x, core).
Axes of the slice: x: 4, y: 8, z: 12, core: 2. Of those that a mesh axis runs over, the one named last changes fastest.
Arguments:
- tokens: bfloat16 [6144, 4096], P('seq', 'head'), may hold values from -24 to 24
- query_weight: bfloat16 [4096, 4096], P('head'), may hold values from -3 to 3
- key_weight: bfloat16 [1024, 4096], P('head'), may hold values from -3 to 3
- value_weight: bfloat16 [1024, 4096], P('head'), may hold values from -0.09375 to 0.09375
- output_weight: bfloat16 [4096, 4096], P('head'), may hold values from -1 to 1
- segments: int32 [6144], replicated, may hold values from 0 to 23, never falling along the last dimension, each value on 1 to 4608 neighbouring positions
Outputs:
- attention_out: bfloat16 [6144, 4096], P('seq', 'head')
The draws below stay inside these ranges and needn't reach their ends.
All inputs are finite; a program needn't handle non-finite values.
Results may differ from the reference program's by a relative error of at most 0.011.
Values may be sent and summed in bfloat16 or wider, within the bound.
No kernel may reach another device: no remote copies, remote signals or barrier semaphores. Data moves between devices by JAX's collectives and lax.ppermute only.
A program may use at most 32 MiB of HBM per device.

```python
import math
import jax
import jax.numpy as jnp
import numpy as np
from jax import lax

D = 4096
HEADS = 32
KV_HEADS = 8
HEAD_DIM = 128
TOKENS = 6144
DOCS = 24
LONGEST = 4608


def draw_tokens(key, part):
    sample = jax.random.normal(jax.random.fold_in(key, 204), (TOKENS, D), jnp.float32)
    return jnp.clip(sample, -6.0, 6.0).astype(jnp.bfloat16)


def draw_query_weight(key, part):
    sample = jax.random.normal(jax.random.fold_in(key, 303), (D, HEADS * HEAD_DIM), jnp.float32)
    return (jnp.clip(sample, -6.0, 6.0) / math.sqrt(D)).T.astype(jnp.bfloat16)


def draw_key_weight(key, part):
    sample = jax.random.normal(jax.random.fold_in(key, 401), (D, KV_HEADS * HEAD_DIM), jnp.float32)
    return (jnp.clip(sample, -6.0, 6.0) / math.sqrt(D)).T.astype(jnp.bfloat16)


def strengthened(entries, key, source, target, blocks, factor):
    def block_of(axis_at):
        return (jnp.arange(entries.shape[axis_at]) // (entries.shape[axis_at] // blocks)).reshape((-1,) + (1,) * (entries.ndim - 1 - axis_at))

    first = jax.random.permutation(key, blocks)[block_of(target)]
    other_side = (block_of(target) + blocks // 2) % blocks
    return jnp.where((block_of(source) == first) | (block_of(source) == other_side), factor * entries, entries)


def steps_of(stream_key, shape, cuts, least, largest):
    gain = 1.0
    for dim, shards_of in cuts:
        heights = jax.random.uniform(jax.random.fold_in(jax.random.fold_in(stream_key, 6), dim), (shards_of,), jnp.float32, least / len(cuts), largest / len(cuts))
        gain = gain * jnp.repeat(jnp.exp(heights), shape[dim] // shards_of).reshape((-1,) + (1,) * (len(shape) - 1 - dim))
    return gain


def length_profile(amount, total, limit, lean):
    portions = [(1 << 20) // math.isqrt(grade ** lean) + 1 for grade in range(2, amount + 1)]
    surplus, counts = total - limit - (amount - 1), [1] * (amount - 1)
    while surplus > 0:
        candidates = [i for i in range(amount - 1) if counts[i] < limit]
        mass, left = sum([portions[i] for i in candidates]), surplus
        for i in candidates:
            addition = min(limit - counts[i], max(1, left * portions[i] // mass), surplus)
            counts[i] = counts[i] + addition
            surplus = surplus - addition
    return np.array([limit] + counts)


def uneven(stream_key, amount, total, bound, skew):
    if amount == 2:
        one = jax.random.randint(stream_key, (), max(1, total - bound), min(bound, total - 1) + 1)
        return jnp.stack([one, total - one])
    lengths = jnp.asarray(length_profile(amount, total, bound, skew), jnp.int32)
    pairs = (amount - 1) // 2
    donor, sink = lengths[1:1 + 2 * pairs:2], lengths[2:2 + 2 * pairs:2]
    room = jnp.minimum(donor - 1, bound - sink)
    moved = jax.random.randint(jax.random.fold_in(stream_key, 1), (pairs,), 0, 1 << 20) % (room + 1)
    lengths = lengths.at[1:1 + 2 * pairs:2].set(donor - moved).at[2:2 + 2 * pairs:2].set(sink + moved)
    return lengths[jax.random.permutation(jax.random.fold_in(stream_key, 2), amount)]


def bell_draw(key, dims, scale, reach, split=(), kind=jnp.bfloat16):
    drawn = jax.random.normal(key, dims, jnp.float32) * scale
    if len(split) > 0:
        drawn = steps_of(key, dims, split, -0.22, 0.18) * drawn
    return jnp.clip(drawn, min=-reach, max=reach).astype(kind)


def gaussian_with(stream_key, extent, scale, bound, shards, heavy, held_as=jnp.bfloat16):
    values = scale * jax.random.normal(stream_key, extent, jnp.float32)
    if shards:
        values = values * steps_of(stream_key, extent, shards, -0.22, 0.18)
    return jnp.clip(strengthened(values, jax.random.fold_in(stream_key, 3), *heavy), -bound, bound).astype(held_as)


def setup_inputs(seed: int = 0) -> dict:
    arg_keys = jax.random.split(jax.random.key(seed), 7)
    return {
        "tokens": draw_tokens(jax.random.fold_in(arg_keys[6], 71), 0),
        "query_weight": draw_query_weight(jax.random.fold_in(arg_keys[6], 71), 0),
        "key_weight": draw_key_weight(jax.random.fold_in(arg_keys[6], 71), 0),
        "value_weight": bell_draw(arg_keys[3], (KV_HEADS * HEAD_DIM, D), D ** -0.5, 0.09375, ((0, 64),)),
        "output_weight": gaussian_with(arg_keys[4], (HEADS * HEAD_DIM, D), (HEADS * HEAD_DIM // 16) ** -0.5, 1.0, ((0, 64),), (0, 1, 64, 4.0)),
        "segments": jnp.searchsorted(jnp.cumsum(uneven(arg_keys[5], DOCS, TOKENS, LONGEST, 0)), jnp.arange(TOKENS), side="right").astype(jnp.int32),
    }


def reference(tokens, query_weight, key_weight, value_weight, output_weight, segments):
    queries = jnp.dot(tokens, query_weight.T, preferred_element_type=jnp.float32).astype(jnp.bfloat16)
    keys = jnp.dot(tokens, key_weight.T, preferred_element_type=jnp.float32).astype(jnp.bfloat16)
    values = jnp.dot(tokens, value_weight.T, preferred_element_type=jnp.float32).astype(jnp.bfloat16)
    position = jnp.arange(TOKENS, dtype=jnp.int32)
    allowed = (segments[:, None] == segments[None, :]) & (position[None, :] <= position[:, None])
    scale = 1.0 / math.sqrt(HEAD_DIM)
    per_shared = HEADS // KV_HEADS

    def one_head(head):
        query_head = lax.dynamic_slice_in_dim(queries, (head * HEAD_DIM).astype(jnp.int32), HEAD_DIM, 1)
        shared = (head // per_shared * HEAD_DIM).astype(jnp.int32)
        key_head = lax.dynamic_slice_in_dim(keys, shared, HEAD_DIM, 1)
        value_head = lax.dynamic_slice_in_dim(values, shared, HEAD_DIM, 1)
        scores = jnp.dot(query_head, key_head.T, preferred_element_type=jnp.float32) * scale
        scores = jnp.where(allowed, scores, -1e+30)
        highest = lax.optimization_barrier(jnp.max(scores, axis=1, keepdims=True))
        powers = jnp.where(allowed, jnp.exp(scores - highest), 0.0)
        totals = lax.optimization_barrier(jnp.sum(powers, axis=1, keepdims=True))
        mixed = jnp.dot(powers.astype(jnp.bfloat16), value_head, preferred_element_type=jnp.float32) / totals
        return mixed.astype(jnp.bfloat16)
    stacked = lax.map(one_head, jnp.arange(HEADS, dtype=jnp.int32))
    attended = jnp.transpose(stacked, (1, 0, 2)).reshape(TOKENS, HEADS * HEAD_DIM)
    width = 2 * HEAD_DIM

    def add_pair(total, index):
        start = (index * width).astype(jnp.int32)
        columns = lax.dynamic_slice_in_dim(attended, start, width, 1)
        weight_rows = lax.dynamic_slice_in_dim(output_weight, start, width, 0)
        part = jnp.dot(columns, weight_rows, preferred_element_type=jnp.float32).astype(jnp.bfloat16)
        part = lax.optimization_barrier(part)
        return (total + part.astype(jnp.float32), None)
    summed, unused = lax.scan(add_pair, jnp.zeros((TOKENS, D), jnp.float32), jnp.arange(HEADS // 2, dtype=jnp.int32))
    return summed.astype(jnp.bfloat16)
```

```python
import functools
import math

import jax
import jax.numpy as jnp
from jax import lax
from jax.experimental import pallas as pl
from jax.experimental.pallas import tpu as pltpu
from jax.sharding import Mesh, PartitionSpec as P

DIM = 128
F32 = jnp.float32
BF16 = jnp.bfloat16
NEG = -1e30
FLOOR = -1e28


def call(body, outs, *args, smem=(), scratch=()):
    specs = [
        pl.BlockSpec(memory_space=pltpu.SMEM if i in smem else pltpu.VMEM)
        for i in range(len(args))
    ]
    single = not isinstance(outs, (list, tuple))
    many = [outs] if single else list(outs)
    out = pl.pallas_call(
        body,
        out_shape=many,
        in_specs=specs,
        out_specs=[pl.BlockSpec(memory_space=pltpu.VMEM)] * len(many),
        scratch_shapes=list(scratch),
    )(*args)
    return out[0] if single else out


def shape(*dims, dtype=BF16):
    return jax.ShapeDtypeStruct(dims, dtype)


def pack_weights(q_ref, k_ref, v_ref, out_ref):
    for x in range(4):
        for y in range(8):
            src = slice((y * 4 + x) * 128, (y * 4 + x + 1) * 128)
            dst = slice(y * 128, (y + 1) * 128)
            out_ref[x, 0:64, dst] = q_ref[:, src]
            out_ref[x, 64:80, dst] = k_ref[:, src]
            out_ref[x, 80:96, dst] = v_ref[:, src]


def pack_output_weight(o_ref, out_ref):
    for y in range(8):
        out_ref[y] = o_ref[:, y * 512 : (y + 1) * 512]


def project(meta_ref, own_ref, other_ref, x_ref, out_ref, y_ref):
    c = meta_ref[2]
    xs = x_ref[...].reshape(1024, 256)
    y_ref[c] = jnp.dot(own_ref[...].reshape(384, 1024), xs, preferred_element_type=F32)
    y_ref[1 - c] = jnp.dot(other_ref[...].reshape(384, 1024), xs, preferred_element_type=F32)
    low = lax.broadcasted_iota(jnp.int32, (16, 128), 1) < 64
    for x in range(4):
        for half in range(2):
            rows = y_ref[half, x * 96 : x * 96 + 64, :]
            for t in range(2):
                at = t * 128 + half * 64
                out_ref[x, at : at + 64, :] = rows[:, t * 128 : (t + 1) * 128].astype(BF16)
    for src in range(4):
        for half in range(2):
            at = 256 + (src * 2 + half) * 16
            for t in range(2):
                lanes = slice(t * 128, (t + 1) * 128)
                key = y_ref[half, src * 96 + 64 : src * 96 + 80, lanes]
                val = y_ref[half, src * 96 + 80 : src * 96 + 96, lanes]
                even = jnp.where(low, key, pltpu.roll(val, 64, 1))
                odd = jnp.where(low, pltpu.roll(key, 64, 1), val)
                out_ref[2 * t, at : at + 16, :] = even.astype(BF16)
                out_ref[2 * t + 1, at : at + 16, :] = odd.astype(BF16)


def sum_projection(in_ref, q_ref, kv_ref):
    total = in_ref[0].astype(F32)
    for j in range(1, 4):
        total = total + in_ref[j].astype(F32)
    total = total.astype(BF16)
    for j in range(4):
        q_ref[j] = total[0:256]
    kv_ref[...] = total[256:384]


def split3(value):
    high = value.astype(BF16)
    rest = value - high.astype(F32)
    mid = rest.astype(BF16)
    low = (rest - mid.astype(F32)).astype(BF16)
    return high, mid, low


def attend(meta_ref, start_ref, q_ref, own_ref, other_ref, out_ref, qs_ref, s_ref, m_ref, o_ref):
    z, x, c, first = meta_ref[0], meta_ref[1], meta_ref[2], meta_ref[3]
    for h in range(4):
        for t in range(2):
            at = (h * 2 + t) * 128
            qs_ref[:, at : at + 128] = q_ref[h, t * 128 : (t + 1) * 128, :]
    begin = jnp.concatenate([start_ref[...]] * 4, axis=1)
    lane = lax.broadcasted_iota(jnp.int32, (1, 1024), 1)
    query = z * 512 + c * 256 + (lane & 255)
    row = lax.broadcasted_iota(jnp.int32, (128, 1), 0)
    offset = (row >> 6) * 256 + x * 64 + (row & 63)
    low = lax.broadcasted_iota(jnp.int32, (128, 128), 1) < 64
    factor = math.log2(math.e) / math.sqrt(DIM)
    m_ref[...] = jnp.full((8, 1024), FLOOR, F32)
    o_ref[...] = jnp.zeros((128, 1024), F32)

    def tiles(j):
        own = own_ref[j].astype(F32)
        other = other_ref[j].astype(F32)
        first_half = jnp.where(c == 0, own, other)
        second_half = jnp.where(c == 0, other, own)
        return first_half, second_half

    def score(j, unused):
        a, b = tiles(j)
        key = jnp.where(low, a, pltpu.roll(b, 64, 1)).T.astype(BF16)
        s = jnp.dot(key, qs_ref[...], preferred_element_type=F32) * factor
        place = j * 512 + offset
        s = jnp.where((place >= begin) & (place <= query), s, NEG)
        s_ref[j] = s
        m_ref[...] = jnp.maximum(m_ref[...], jnp.max(s.reshape(16, 8, 1024), axis=0))
        return unused

    lax.fori_loop(first, z + 1, score, 0)
    top = jnp.max(m_ref[...], axis=0, keepdims=True)

    def mix(j, total):
        a, b = tiles(j)
        val = jnp.where(low, pltpu.roll(a, 64, 1), b).astype(BF16)
        p = jnp.exp2(s_ref[j] - top)
        o_ref[...] += jnp.dot(val, p.astype(BF16), preferred_element_type=F32)
        return total + jnp.sum(p.reshape(16, 8, 1024), axis=0)

    total = lax.fori_loop(first, z + 1, mix, jnp.zeros((8, 1024), F32))
    total = jnp.sum(total, axis=0, keepdims=True)
    stats = [v.astype(F32) for v in split3(top) + split3(total)]
    stats = jnp.concatenate(stats + [jnp.zeros((2, 1024), F32)], axis=0)
    for h in range(4):
        lanes = slice(h * 256, (h + 1) * 256)
        out_ref[h, 0:128, :] = o_ref[:, lanes].astype(BF16)
        out_ref[h, 128:136, :] = stats[:, lanes].astype(BF16)


def combine(in_ref, out_ref):
    tops, totals = [], []
    for j in range(4):
        st = in_ref[j, 128:136, :].astype(F32)
        tops.append(st[0:1] + st[1:2] + st[2:3])
        totals.append(st[3:4] + st[4:5] + st[5:6])
    top = jnp.maximum(jnp.maximum(tops[0], tops[1]), jnp.maximum(tops[2], tops[3]))
    shares = [jnp.exp2(t - top) for t in tops]
    total = sum(w * t for w, t in zip(shares, totals))
    mixed = sum(in_ref[j, 0:128, :].astype(F32) * (shares[j] / total) for j in range(4))
    mixed = mixed.astype(BF16)
    for j in range(8):
        out_ref[j] = mixed


def output_project(meta_ref, own_ref, other_ref, a_ref, out_ref, one_ref, two_ref):
    c = meta_ref[2]
    for y in range(8):
        one_ref[y * 64 : (y + 1) * 64, :] = a_ref[y, pl.ds(pl.multiple_of(c * 64, 64), 64), :]
        two_ref[y * 64 : (y + 1) * 64, :] = a_ref[y, pl.ds(pl.multiple_of(64 - c * 64, 64), 64), :]
    dims = (((0,), (0,)), ((), ()))
    r = lax.dot_general(own_ref[...].reshape(512, 512), one_ref[...], dims, preferred_element_type=F32)
    r = r + lax.dot_general(other_ref[...].reshape(512, 512), two_ref[...], dims, preferred_element_type=F32)
    out_ref[...] = r.astype(BF16).reshape(4, 128, 256)


def sum_output(in_ref, out_ref):
    total = in_ref[0].astype(F32)
    for j in range(1, 4):
        total = total + in_ref[j].astype(F32)
    out_ref[...] = total.astype(BF16).reshape(2, 64, 256)


def trade(block, axis):
    return lax.all_to_all(block, axis, split_axis=0, concat_axis=0, tiled=True)


def partner(block):
    return lax.ppermute(block, "c", [(0, 1), (1, 0)])


def local(tokens, query_weight, key_weight, value_weight, output_weight, segments):
    z, x, c = lax.axis_index("z"), lax.axis_index("x"), lax.axis_index("c")
    first_query = z * 512 + c * 256
    segment = lax.dynamic_slice_in_dim(segments, first_query, 256, 0)
    starts = jnp.sum((segments[:, None] < segment[None, :]).astype(jnp.int32), axis=0)
    place = lax.iota(jnp.int32, 8)
    meta = jnp.where(
        place == 0, z, jnp.where(place == 1, x, jnp.where(place == 2, c, starts[0] // 512))
    )

    halves = tokens.T.reshape(64, 2, 256).transpose(1, 0, 2)
    columns = trade(halves, "c").reshape(1, 128, 256)
    columns = trade(jnp.broadcast_to(columns, (8, 128, 256)), "y")

    packed = call(pack_weights, shape(4, 96, 1024), query_weight, key_weight, value_weight)
    own = trade(packed, "x")
    other = partner(own)

    out_own = trade(call(pack_output_weight, shape(8, 64, 512), output_weight), "y")
    out_other = partner(out_own)

    partial = call(
        project, shape(4, 384, 128), meta, own, other, columns, smem=(0,),
        scratch=[pltpu.VMEM((2, 384, 256), F32)],
    )
    spread, kv = call(sum_projection, [shape(4, 256, 128), shape(128, 128)], trade(partial, "x"))
    queries = trade(spread, "x")
    kv_own = lax.all_gather(kv, "z", axis=0, tiled=False)
    kv_other = partner(kv_own)
    mixed = call(
        attend, shape(4, 136, 256), meta, starts.reshape(1, 256), queries, kv_own, kv_other,
        smem=(0,),
        scratch=[
            pltpu.VMEM((128, 1024), BF16),
            pltpu.VMEM((12, 128, 1024), F32),
            pltpu.VMEM((8, 1024), F32),
            pltpu.VMEM((128, 1024), F32),
        ],
    )
    attended = trade(call(combine, shape(8, 128, 256), trade(mixed, "x")), "y")
    result = call(
        output_project, shape(4, 128, 256), meta, out_own, out_other, attended, smem=(0,),
        scratch=[pltpu.VMEM((512, 256), BF16), pltpu.VMEM((512, 256), BF16)],
    )
    summed = call(sum_output, shape(2, 64, 256), trade(result, "x"))
    final = trade(summed, "c")
    return final.transpose(1, 0, 2).reshape(64, 512).T


def solution(mesh):
    grid = Mesh(mesh.devices.reshape(12, 8, 4, 2), ("z", "y", "x", "c"))
    head = ("y", "x", "c")
    placed = (P("z", head), P(head, None), P(head, None), P(head, None), P(head, None), P())
    return jax.shard_map(
        local, mesh=grid, in_specs=placed, out_specs=P("z", head), check_vma=False
    )
```

```python
import math

import jax
import jax.numpy as jnp
from jax import lax
from jax.experimental import pallas as pl
from jax.experimental.pallas import tpu as pltpu
from jax.sharding import Mesh, PartitionSpec as P


DIM = 128
F32 = jnp.float32
BF16 = jnp.bfloat16
NEG = -1e30
FLOOR = -1e28


def call(body, outs, *args, smem=(), scratch=(), limit=8):
    specs = [
        pl.BlockSpec(memory_space=pltpu.SMEM if i in smem else pltpu.VMEM)
        for i in range(len(args))
    ]
    single = not isinstance(outs, (list, tuple))
    many = [outs] if single else list(outs)
    out = pl.pallas_call(
        body,
        out_shape=many,
        in_specs=specs,
        out_specs=[pl.BlockSpec(memory_space=pltpu.VMEM)] * len(many),
        scratch_shapes=list(scratch),
        compiler_params=pltpu.CompilerParams(vmem_limit_bytes=limit << 20),
    )(*args)
    return out[0] if single else out


def shape(*dims, dtype=BF16):
    return jax.ShapeDtypeStruct(dims, dtype)


def find_starts(meta_ref, seg_ref, start_ref, first_ref):
    at = meta_ref[0] * 2 + meta_ref[2]
    window = seg_ref[pl.ds(at, 1), :]
    lane = lax.broadcasted_iota(jnp.int32, (1, 256), 1)
    head = jnp.min(window)
    begin = jnp.sum((seg_ref[...] < head).astype(jnp.int32))
    changed = (lane > 0) & (window != pltpu.roll(window, 1, 1))
    starts = jnp.where(changed, at * 256 + lane, begin)
    for bit in range(8):
        moved = pltpu.roll(starts, 1 << bit, 1)
        starts = jnp.maximum(starts, jnp.where(lane >= 1 << bit, moved, 0))
    start_ref[...] = starts
    first_ref[0] = begin


def away(x, step):
    return (x + step) & 3


def pack_weights(meta_ref, q_ref, k_ref, v_ref, o_ref, *outs):
    for step in range(4):
        x = away(meta_ref[1], step)
        w_ref, out_ref = outs[step], outs[4 + step]
        for y in range(8):
            src = pl.ds(pl.multiple_of((y * 4 + x) * 128, 128), 128)
            dst = slice(y * 128, (y + 1) * 128)
            w_ref[0:64, dst] = q_ref[:, src]
            w_ref[64:80, dst] = k_ref[:, src]
            w_ref[80:96, dst] = v_ref[:, src]
            out_ref[:, dst] = o_ref[:, src]


def take_columns(meta_ref, in_ref, out_ref):
    c = meta_ref[2]
    for half in range(2):
        block = jnp.where(c == 0, in_ref[half, 0:64, :], in_ref[half, 64:128, :])
        out_ref[:, half * 256 : (half + 1) * 256] = block


def rows_of(start, size):
    return pl.ds(pl.multiple_of(start, size), size)


def project(meta_ref, w0, w1, w2, w3, own_ref, other_ref, *rest):
    outs, (x_ref, all_ref, y_ref) = rest[:4], rest[4:]
    x, c = meta_ref[1], meta_ref[2]
    for y in range(8):
        x_ref[rows_of(y * 128 + c * 64, 64), :] = own_ref[y * 64 : (y + 1) * 64, :]
        x_ref[rows_of(y * 128 + 64 - c * 64, 64), :] = other_ref[y * 64 : (y + 1) * 64, :]
    for step, w in enumerate((w0, w1, w2, w3)):
        all_ref[pl.ds(pl.multiple_of(away(x, -step) * 96, 32), 96), :] = w[...]
    y_ref[...] = jnp.dot(all_ref[...], x_ref[...], preferred_element_type=F32)
    for step, out_ref in enumerate(outs):
        to = away(x, step)
        rows = y_ref[pl.ds(pl.multiple_of(to * 96, 32), 64), :].astype(BF16)
        for t in range(4):
            out_ref[t * 64 : (t + 1) * 64, :] = rows[:, t * 128 : (t + 1) * 128]
        lanes = pl.ds(pl.multiple_of(to * 128, 128), 128)
        for j in range(4):
            at = 256 + j * 16
            out_ref[at : at + 16, :] = y_ref[j * 96 + 64 : j * 96 + 80, lanes].astype(BF16)
            at = 320 + j * 16
            out_ref[at : at + 16, :] = y_ref[j * 96 + 80 : j * 96 + 96, lanes].astype(BF16)


def sum_projection(a_ref, b_ref, c_ref, d_ref, q_ref, kv_ref):
    total = a_ref[...].astype(F32) + b_ref[...].astype(F32)
    total = (total + c_ref[...].astype(F32) + d_ref[...].astype(F32)).astype(BF16)
    q_ref[...] = total[0:256]
    for j in range(12):
        kv_ref[j] = total[256:384]


def split3(value):
    high = value.astype(BF16)
    rest = value - high.astype(F32)
    mid = rest.astype(BF16)
    low = (rest - mid.astype(F32)).astype(BF16)
    return high, mid, low


def attend(meta_ref, first_ref, start_ref, q_ref, kv_ref, out0, out1, out2, out3, qs_ref, s_ref, m_ref, o_ref, st_ref):
    z, x, c, first = meta_ref[0], meta_ref[1], meta_ref[2], first_ref[0] >> 9
    for h in range(4):
        for t in range(2):
            lanes = slice((h * 2 + t) * 128, (h * 2 + t + 1) * 128)
            for block in range(8):
                to = (block % 2) * 64 + (block // 2) * 16
                at = pl.ds(pl.multiple_of(c * 128 + t * 64 + (block % 4) * 16, 16), 16)
                qs_ref[to : to + 16, lanes] = q_ref[h * 2 + block // 4, at, :]
    begin = jnp.concatenate([start_ref[...]] * 4, axis=1)
    lane = lax.broadcasted_iota(jnp.int32, (1, 1024), 1)
    query = z * 512 + c * 256 + (lane & 255)
    offset = lax.broadcasted_iota(jnp.int32, (128, 1), 0) + x * 128
    factor = math.log2(math.e) / math.sqrt(DIM)
    m_ref[...] = jnp.full((8, 1024), FLOOR, F32)
    o_ref[...] = jnp.zeros((128, 1024), F32)

    def score(j, unused):
        key = jnp.concatenate([kv_ref[0, j, 0:64, :], kv_ref[1, j, 0:64, :]], axis=0)
        key = key.astype(F32).T.astype(BF16)
        s = jnp.dot(key, qs_ref[...], preferred_element_type=F32) * factor
        place = j * 512 + offset
        s = jnp.where((place >= begin) & (place <= query), s, NEG)
        s_ref[j] = s
        m_ref[...] = jnp.maximum(m_ref[...], jnp.max(s.reshape(16, 8, 1024), axis=0))
        return unused

    lax.fori_loop(first, z + 1, score, 0)
    top = jnp.max(m_ref[...], axis=0, keepdims=True)

    def mix(j, total):
        val = jnp.concatenate([kv_ref[0, j, 64:128, :], kv_ref[1, j, 64:128, :]], axis=0)
        p = jnp.exp2(s_ref[j] - top)
        o_ref[...] += jnp.dot(val, p.astype(BF16), preferred_element_type=F32)
        return total + jnp.sum(p.reshape(16, 8, 1024), axis=0)

    total = lax.fori_loop(first, z + 1, mix, jnp.zeros((8, 1024), F32))
    total = jnp.sum(total, axis=0, keepdims=True)
    stats = [v.astype(F32) for v in split3(top) + split3(total)]
    stats = jnp.concatenate(stats + [jnp.zeros((2, 1024), F32)], axis=0)
    st_ref[...] = stats
    for step, out_ref in enumerate((out0, out1, out2, out3)):
        lanes = pl.ds(pl.multiple_of(away(x, step) * 256, 256), 256)
        for block in range(8):
            at = (block % 2) * 64 + (block // 2) * 16
            out_ref[block * 16 : block * 16 + 16, :] = o_ref[at : at + 16, lanes].astype(BF16)
        out_ref[128:136, :] = st_ref[:, lanes].astype(BF16)


def combine(a_ref, b_ref, c_ref, d_ref, out_ref):
    parts = (a_ref, b_ref, c_ref, d_ref)
    tops, totals = [], []
    for part in parts:
        st = part[128:136, :].astype(F32)
        tops.append(st[0:1] + st[1:2] + st[2:3])
        totals.append(st[3:4] + st[4:5] + st[5:6])
    top = jnp.maximum(jnp.maximum(tops[0], tops[1]), jnp.maximum(tops[2], tops[3]))
    shares = [jnp.exp2(t - top) for t in tops]
    total = sum(w * t for w, t in zip(shares, totals))
    mixed = sum(p[0:128, :].astype(F32) * (w / total) for p, w in zip(parts, shares))
    out_ref[...] = mixed.astype(BF16)


def output_project(meta_ref, own_ref, other_ref, a0, a1, a2, a3, out_ref, o_ref, a_ref):
    x, c = meta_ref[1], meta_ref[2]
    for step, part in enumerate((a0, a1, a2, a3)):
        at = away(x, -step) * 128
        a_ref[rows_of(at, 128), :] = part[...]
        o_ref[rows_of(at + c * 64, 64), :] = own_ref[step]
        o_ref[rows_of(at + 64 - c * 64, 64), :] = other_ref[step]
    dims = (((0,), (0,)), ((), ()))
    r = lax.dot_general(o_ref[...], a_ref[...], dims, preferred_element_type=F32)
    out_ref[...] = r.astype(BF16).reshape(8, 128, 256)


def sum_output(in_ref, out_ref):
    total = in_ref[0].astype(F32)
    for j in range(1, 8):
        total = total + in_ref[j].astype(F32)
    out_ref[...] = total.astype(BF16)


def trade(block, axis):
    return lax.all_to_all(block, axis, split_axis=0, concat_axis=0, tiled=True)


def gather(block, axis):
    return lax.all_gather(block, axis, axis=0, tiled=False)


def send(block, step):
    if step == 0:
        return block
    return lax.ppermute(block, "x", [(i, (i + step) % 4) for i in range(4)])


def partner(block):
    return lax.ppermute(block, "c", [(0, 1), (1, 0)])


def layer(tokens, query_weight, key_weight, value_weight, output_weight, segments):
    z, x, c = lax.axis_index("z"), lax.axis_index("x"), lax.axis_index("c")
    place = lax.iota(jnp.int32, 4)
    meta = jnp.where(place == 0, z, jnp.where(place == 1, x, c))
    starts, first = pl.pallas_call(
        find_starts,
        out_shape=[shape(1, 256, dtype=jnp.int32), shape(1, dtype=jnp.int32)],
        in_specs=[pl.BlockSpec(memory_space=s) for s in (pltpu.SMEM, pltpu.VMEM)],
        out_specs=[pl.BlockSpec(memory_space=s) for s in (pltpu.VMEM, pltpu.SMEM)],
        scratch_shapes=[],
        compiler_params=pltpu.CompilerParams(vmem_limit_bytes=4 << 20),
    )(meta, segments.reshape(24, 256))
    own = trade(jnp.broadcast_to(tokens.T, (8, 64, 512)), "y").reshape(512, 512)
    packed = call(
        pack_weights, [shape(96, 1024)] * 4 + [shape(64, 1024)] * 4,
        meta, query_weight, key_weight, value_weight, output_weight, smem=(0,),
    )
    weights = [send(packed[i], i) for i in range(4)]
    o_own = jnp.stack([send(packed[4 + i], i) for i in range(4)])
    o_other = partner(o_own)
    other = partner(own)
    partial = call(
        project, [shape(384, 128)] * 4, meta, *weights, own, other, smem=(0,), limit=12,
        scratch=[
            pltpu.VMEM((1024, 512), BF16),
            pltpu.VMEM((384, 1024), BF16),
            pltpu.VMEM((384, 512), F32),
        ],
    )
    partial = [send(partial[i], i) for i in range(4)]
    queries, spread = call(sum_projection, [shape(256, 128), shape(12, 128, 128)], *partial)
    memory = trade(spread, "z")
    queries = gather(queries, ("x", "c"))
    memory = gather(memory, "c")
    mixed = call(
        attend, [shape(136, 256)] * 4, meta, first, starts, queries, memory,
        smem=(0, 1),
        limit=16,
        scratch=[
            pltpu.VMEM((128, 1024), BF16),
            pltpu.VMEM((12, 128, 1024), F32),
            pltpu.VMEM((8, 1024), F32),
            pltpu.VMEM((128, 1024), F32),
            pltpu.VMEM((8, 1024), F32),
        ],
    )
    mixed = [send(mixed[i], i) for i in range(4)]
    attended = call(combine, shape(128, 256), *mixed)
    attended = [send(attended, i) for i in range(4)]
    result = call(
        output_project, shape(8, 128, 256), meta, o_own, o_other, *attended, smem=(0,), limit=12,
        scratch=[pltpu.VMEM((512, 1024), BF16), pltpu.VMEM((512, 256), BF16)],
    )
    summed = call(sum_output, shape(128, 256), trade(result, "y"))
    final = call(take_columns, shape(64, 512), meta, gather(summed, "c"), smem=(0,))
    return final.T


def solution(mesh):
    grid = Mesh(mesh.devices.reshape(12, 8, 4, 2), ("z", "y", "x", "c"))
    head = ("y", "x", "c")
    placed = (P("z", head), P(head, None), P(head, None), P(head, None), P(head, None), P())
    return jax.shard_map(layer, mesh=grid, in_specs=placed, out_specs=P("z", head), check_vma=False)
```

```python
import math

import jax
import jax.numpy as jnp
from jax import lax
from jax.experimental import pallas as pl
from jax.experimental.pallas import tpu as pltpu
from jax.sharding import Mesh, PartitionSpec as P


DIM = 128
F32 = jnp.float32
BF16 = jnp.bfloat16
NEG = -1e30
FLOOR = -1e28


def call(body, outs, *args, smem=(), scratch=(), limit=8):
    specs = [
        pl.BlockSpec(memory_space=pltpu.SMEM if i in smem else pltpu.VMEM)
        for i in range(len(args))
    ]
    single = not isinstance(outs, (list, tuple))
    many = [outs] if single else list(outs)
    out = pl.pallas_call(
        body,
        out_shape=many,
        in_specs=specs,
        out_specs=[pl.BlockSpec(memory_space=pltpu.VMEM)] * len(many),
        scratch_shapes=list(scratch),
        compiler_params=pltpu.CompilerParams(vmem_limit_bytes=limit << 20),
    )(*args)
    return out[0] if single else out


def shape(*dims, dtype=BF16):
    return jax.ShapeDtypeStruct(dims, dtype)


def find_starts(meta_ref, seg_ref, start_ref, first_ref):
    at = meta_ref[0] * 2 + meta_ref[2]
    window = seg_ref[pl.ds(at, 1), :]
    lane = lax.broadcasted_iota(jnp.int32, (1, 256), 1)
    head = jnp.min(window)
    begin = jnp.sum((seg_ref[...] < head).astype(jnp.int32))
    changed = (lane > 0) & (window != pltpu.roll(window, 1, 1))
    starts = jnp.where(changed, at * 256 + lane, begin)
    for bit in range(8):
        moved = pltpu.roll(starts, 1 << bit, 1)
        starts = jnp.maximum(starts, jnp.where(lane >= 1 << bit, moved, 0))
    start_ref[...] = starts
    first_ref[0] = begin
    first_ref[1] = jnp.max(starts)


def away(x, step):
    return (x + step) & 3


def pack_weights(meta_ref, q_ref, k_ref, v_ref, o_ref, *outs):
    for step, out_ref in enumerate(outs):
        x = away(meta_ref[1], step)
        for y in range(8):
            src = pl.ds(pl.multiple_of((y * 4 + x) * 128, 128), 128)
            dst = slice(y * 128, (y + 1) * 128)
            out_ref[0:64, dst] = q_ref[:, src]
            out_ref[64:80, dst] = k_ref[:, src]
            out_ref[80:96, dst] = v_ref[:, src]
            out_ref[96:160, dst] = o_ref[:, src]


def rows_of(start, size):
    return pl.ds(pl.multiple_of(start, size), size)


def project(meta_ref, w0, w1, w2, w3, own_ref, other_ref, out_ref, o_ref, x_ref, all_ref, y_ref):
    x, c = meta_ref[1], meta_ref[2]
    for y in range(8):
        x_ref[rows_of(y * 128 + c * 64, 64), :] = own_ref[y * 64 : (y + 1) * 64, :]
        x_ref[rows_of(y * 128 + 64 - c * 64, 64), :] = other_ref[y * 64 : (y + 1) * 64, :]
    for step, w in enumerate((w0, w1, w2, w3)):
        all_ref[pl.ds(pl.multiple_of(away(x, -step) * 96, 32), 96), :] = w[0:96, :]
        o_ref[step] = w[96:160, :]
    y_ref[...] = jnp.dot(all_ref[...], x_ref[...], preferred_element_type=F32).astype(BF16)
    for j in range(4):
        for t in range(4):
            lanes = slice(t * 128, (t + 1) * 128)
            at = (t % 2) * 64
            out_ref[j * 2 + t // 2, at : at + 64, :] = y_ref[j * 96 : j * 96 + 64, lanes]
            at = 128 + j * 16
            out_ref[t * 2, at : at + 16, :] = y_ref[j * 96 + 64 : j * 96 + 80, lanes]
            out_ref[t * 2 + 1, at : at + 16, :] = y_ref[j * 96 + 80 : j * 96 + 96, lanes]


def sum_projection(in_ref, q_ref, kv_ref):
    for half in range(2):
        total = in_ref[half].astype(F32)
        for j in range(1, 4):
            total = total + in_ref[j * 2 + half].astype(F32)
        total = total.astype(BF16)
        rows = slice(half * 64, half * 64 + 64)
        for t in range(2):
            q_ref[t, rows, :] = total[t * 64 : t * 64 + 64]
        for j in range(12):
            kv_ref[j, rows, :] = total[128:192]


def split3(value):
    high = value.astype(BF16)
    rest = value - high.astype(F32)
    mid = rest.astype(BF16)
    low = (rest - mid.astype(F32)).astype(BF16)
    return high, mid, low


def attend(meta_ref, first_ref, start_ref, q_ref, kv_ref, out_ref, qs_ref, s_ref, m_ref, l_ref, o_ref):
    z, x, c = meta_ref[0], meta_ref[1], meta_ref[2]
    first, latest = first_ref[0] >> 9, first_ref[1]
    for block in range(8):
        to = (block % 2) * 64 + (block // 2) * 16
        for h in range(4):
            for t in range(2):
                lanes = slice((h * 2 + t) * 128, (h * 2 + t + 1) * 128)
                qs_ref[to : to + 16, lanes] = q_ref[h, t, block * 16 : block * 16 + 16, :]
    factor = math.log2(math.e) / math.sqrt(DIM)
    m_ref[...] = jnp.full((8, 1024), FLOOR, F32)
    l_ref[...] = jnp.zeros((8, 1024), F32)
    o_ref[...] = jnp.zeros((128, 1024), F32)
    heads = [slice(h * 256, (h + 1) * 256) for h in range(4)]
    pairs = (z - first + 2) >> 1

    def tile(which, i):
        j = first + 2 * i
        return jnp.concatenate([kv_ref[which, j], kv_ref[which, jnp.minimum(j + 1, 11)]], axis=1)

    def score(i, unused):
        j = first + 2 * i
        key = tile(0, i).astype(F32).T.astype(BF16)

        def note(s, lanes):
            s_ref[i, :, lanes] = s
            m_ref[:, lanes] = jnp.maximum(m_ref[:, lanes], jnp.max(s.reshape(32, 8, 256), axis=0))

        inside = (j * 512 >= latest) & (j + 1 < z)

        @pl.when(inside)
        def _():
            for lanes in heads:
                note(jnp.dot(key, qs_ref[:, lanes], preferred_element_type=F32) * factor, lanes)

        @pl.when(jnp.logical_not(inside))
        def _():
            row = lax.broadcasted_iota(jnp.int32, (256, 256), 0)
            place = j * 512 + (row >> 7) * 512 + x * 128 + (row & 127)
            query = z * 512 + c * 256 + lax.broadcasted_iota(jnp.int32, (256, 256), 1)
            allowed = (place >= start_ref[...]) & (place <= query)
            for lanes in heads:
                s = jnp.dot(key, qs_ref[:, lanes], preferred_element_type=F32) * factor
                note(jnp.where(allowed, s, NEG), lanes)

        return unused

    lax.fori_loop(0, pairs, score, 0)
    top = jnp.max(m_ref[...], axis=0, keepdims=True)

    def mix(i, unused):
        val = tile(1, i)
        for lanes in heads:
            p = jnp.exp2(s_ref[i, :, lanes] - top[:, lanes])
            l_ref[:, lanes] += jnp.sum(p.reshape(32, 8, 256), axis=0)
            o_ref[:, lanes] += jnp.dot(val, p.astype(BF16), preferred_element_type=F32)
        return unused

    lax.fori_loop(0, pairs, mix, 0)
    total = jnp.sum(l_ref[...], axis=0, keepdims=True)
    stats = [v.astype(F32) for v in split3(top) + split3(total)]
    stats = jnp.concatenate(stats + [jnp.zeros((2, 1024), F32)], axis=0)
    for h, lanes in enumerate(heads):
        for block in range(8):
            at = (block % 2) * 64 + (block // 2) * 16
            out_ref[h, block * 16 : block * 16 + 16, :] = o_ref[at : at + 16, lanes].astype(BF16)
        out_ref[h, 128:136, :] = stats[:, lanes].astype(BF16)


def combine(in_ref, out_ref):
    tops, totals = [], []
    for j in range(4):
        st = in_ref[j, 128:136, :].astype(F32)
        tops.append(st[0:1] + st[1:2] + st[2:3])
        totals.append(st[3:4] + st[4:5] + st[5:6])
    top = jnp.maximum(jnp.maximum(tops[0], tops[1]), jnp.maximum(tops[2], tops[3]))
    shares = [jnp.exp2(t - top) for t in tops]
    total = sum(w * t for w, t in zip(shares, totals))
    mixed = sum(in_ref[j, 0:128, :].astype(F32) * (shares[j] / total) for j in range(4))
    mixed = mixed.astype(BF16)
    for j in range(4):
        out_ref[j] = mixed


def output_project(meta_ref, own_ref, other_ref, a_ref, out_ref, o_ref):
    x, c = meta_ref[1], meta_ref[2]
    for step in range(4):
        at = away(x, -step) * 128
        o_ref[rows_of(at + c * 64, 64), :] = own_ref[step]
        o_ref[rows_of(at + 64 - c * 64, 64), :] = other_ref[step]
    dims = (((0,), (0,)), ((), ()))
    r = lax.dot_general(o_ref[...], a_ref[...].reshape(512, 256), dims, preferred_element_type=F32)
    out_ref[...] = r.astype(BF16).reshape(16, 64, 256)


def sum_output(in_ref, out_ref):
    for half in range(2):
        total = in_ref[half].astype(F32)
        for j in range(1, 8):
            total = total + in_ref[j * 2 + half].astype(F32)
        out_ref[:, half * 256 : (half + 1) * 256] = total.astype(BF16)


def trade(block, axis):
    return lax.all_to_all(block, axis, split_axis=0, concat_axis=0, tiled=True)


def gather(block, axis):
    return lax.all_gather(block, axis, axis=0, tiled=False)


def send(block, step):
    if step == 0:
        return block
    return lax.ppermute(block, "x", [(i, (i + step) % 4) for i in range(4)])


def partner(block):
    return lax.ppermute(block, "c", [(0, 1), (1, 0)])


def layer(tokens, query_weight, key_weight, value_weight, output_weight, segments):
    z, x, c = lax.axis_index("z"), lax.axis_index("x"), lax.axis_index("c")
    place = lax.iota(jnp.int32, 4)
    meta = jnp.where(place == 0, z, jnp.where(place == 1, x, c))
    starts, first = pl.pallas_call(
        find_starts,
        out_shape=[shape(1, 256, dtype=jnp.int32), shape(2, dtype=jnp.int32)],
        in_specs=[pl.BlockSpec(memory_space=s) for s in (pltpu.SMEM, pltpu.VMEM)],
        out_specs=[pl.BlockSpec(memory_space=s) for s in (pltpu.VMEM, pltpu.SMEM)],
        scratch_shapes=[],
        compiler_params=pltpu.CompilerParams(vmem_limit_bytes=4 << 20),
    )(meta, segments.reshape(24, 256))
    own = trade(jnp.broadcast_to(tokens.T, (8, 64, 512)), "y").reshape(512, 512)
    packed = call(
        pack_weights, [shape(160, 1024)] * 4,
        meta, query_weight, key_weight, value_weight, output_weight, smem=(0,),
    )
    weights = [send(packed[i], i) for i in range(4)]
    other = partner(own)
    partial, o_own = call(
        project, [shape(8, 192, 128), shape(4, 64, 1024)],
        meta, *weights, own, other, smem=(0,), limit=12,
        scratch=[
            pltpu.VMEM((1024, 512), BF16),
            pltpu.VMEM((384, 1024), BF16),
            pltpu.VMEM((384, 512), BF16),
        ],
    )
    o_other = partner(o_own)
    queries, spread = call(
        sum_projection,
        [shape(2, 128, 128), shape(12, 128, 128)],
        trade(partial, ("x", "c")),
    )
    memory = trade(spread, "z")
    queries = gather(queries, "x")
    memory = gather(memory, "c")
    mixed = call(
        attend, shape(4, 136, 256), meta, first, starts, queries, memory,
        smem=(0, 1),
        limit=16,
        scratch=[
            pltpu.VMEM((128, 1024), BF16),
            pltpu.VMEM((6, 256, 1024), F32),
            pltpu.VMEM((8, 1024), F32),
            pltpu.VMEM((8, 1024), F32),
            pltpu.VMEM((128, 1024), F32),
        ],
    )
    attended = trade(call(combine, shape(4, 128, 256), trade(mixed, "x")), "x")
    result = call(
        output_project, shape(16, 64, 256), meta, o_own, o_other, attended, smem=(0,), limit=12,
        scratch=[pltpu.VMEM((512, 1024), BF16)],
    )
    final = call(sum_output, shape(64, 512), trade(result, ("y", "c")))
    return final.T


def solution(mesh):
    grid = Mesh(mesh.devices.reshape(12, 8, 4, 2), ("z", "y", "x", "c"))
    head = ("y", "x", "c")
    placed = (P("z", head), P(head, None), P(head, None), P(head, None), P(head, None), P())
    return jax.shard_map(layer, mesh=grid, in_specs=placed, out_specs=P("z", head), check_vma=False)
```

```python
import math

import jax
import jax.numpy as jnp
from jax import lax
from jax.experimental import pallas as pl
from jax.experimental.pallas import tpu as pltpu
from jax.sharding import Mesh, PartitionSpec as P


DIM = 128
F32 = jnp.float32
BF16 = jnp.bfloat16
NEG = -1e30
FLOOR = -1e28


def call(body, outs, *args, smem=(), scratch=(), limit=8):
    specs = [
        pl.BlockSpec(memory_space=pltpu.SMEM if i in smem else pltpu.VMEM)
        for i in range(len(args))
    ]
    single = not isinstance(outs, (list, tuple))
    many = [outs] if single else list(outs)
    out = pl.pallas_call(
        body,
        out_shape=many,
        in_specs=specs,
        out_specs=[pl.BlockSpec(memory_space=pltpu.VMEM)] * len(many),
        scratch_shapes=list(scratch),
        compiler_params=pltpu.CompilerParams(vmem_limit_bytes=limit << 20),
    )(*args)
    return out[0] if single else out


def shape(*dims, dtype=BF16):
    return jax.ShapeDtypeStruct(dims, dtype)


def find_starts(meta_ref, seg_ref, start_ref, first_ref):
    at = meta_ref[0] * 2 + meta_ref[2]
    window = seg_ref[pl.ds(at, 1), :]
    lane = lax.broadcasted_iota(jnp.int32, (1, 256), 1)
    head = jnp.min(window)
    begin = jnp.sum((seg_ref[...] < head).astype(jnp.int32))
    changed = (lane > 0) & (window != pltpu.roll(window, 1, 1))
    starts = jnp.where(changed, at * 256 + lane, begin)
    for bit in range(8):
        moved = pltpu.roll(starts, 1 << bit, 1)
        starts = jnp.maximum(starts, jnp.where(lane >= 1 << bit, moved, 0))
    start_ref[...] = starts
    first_ref[0] = begin
    first_ref[1] = jnp.max(starts)


def away(x, step):
    return (x + step) & 3


def pack_weights(meta_ref, q_ref, k_ref, v_ref, o_ref, *outs):
    for step, out_ref in enumerate(outs):
        x = away(meta_ref[1], step)
        for y in range(8):
            src = pl.ds(pl.multiple_of((y * 4 + x) * 128, 128), 128)
            dst = slice(y * 128, (y + 1) * 128)
            out_ref[0:64, dst] = q_ref[:, src]
            out_ref[64:80, dst] = k_ref[:, src]
            out_ref[80:96, dst] = v_ref[:, src]
            out_ref[96:160, dst] = o_ref[:, src]


def rows_of(start, size):
    return pl.ds(pl.multiple_of(start, size), size)


def project(meta_ref, w0, w1, w2, w3, own_ref, other_ref, out_ref, o_ref, x_ref, all_ref, y_ref):
    x, c = meta_ref[1], meta_ref[2]
    for y in range(8):
        x_ref[rows_of(y * 128 + c * 64, 64), :] = own_ref[y * 64 : (y + 1) * 64, :]
        x_ref[rows_of(y * 128 + 64 - c * 64, 64), :] = other_ref[y * 64 : (y + 1) * 64, :]
    for step, w in enumerate((w0, w1, w2, w3)):
        all_ref[pl.ds(pl.multiple_of(away(x, -step) * 96, 32), 96), :] = w[0:96, :]
        o_ref[step] = w[96:160, :]
    y_ref[...] = jnp.dot(all_ref[...], x_ref[...], preferred_element_type=F32).astype(BF16)
    for j in range(4):
        for t in range(4):
            lanes = slice(t * 128, (t + 1) * 128)
            out_ref[j, t * 64 : (t + 1) * 64, :] = y_ref[j * 96 : j * 96 + 64, lanes]
            at = 256 + j * 16
            out_ref[t, at : at + 16, :] = y_ref[j * 96 + 64 : j * 96 + 80, lanes]
            at = 320 + j * 16
            out_ref[t, at : at + 16, :] = y_ref[j * 96 + 80 : j * 96 + 96, lanes]


def sum_projection(in_ref, q_ref, kv_ref):
    total = in_ref[0].astype(F32)
    for j in range(1, 4):
        total = total + in_ref[j].astype(F32)
    total = total.astype(BF16)
    q_ref[...] = total[0:256]
    for j in range(12):
        kv_ref[j] = total[256:384]


def spread_tokens(in_ref, out_ref, sems):
    copies = [pltpu.make_async_copy(in_ref, out_ref.at[y], sems.at[y]) for y in range(8)]
    for copy in copies:
        copy.start()
    for copy in copies:
        copy.wait()


def split3(value):
    high = value.astype(BF16)
    rest = value - high.astype(F32)
    mid = rest.astype(BF16)
    low = (rest - mid.astype(F32)).astype(BF16)
    return high, mid, low


def attend(meta_ref, first_ref, start_ref, q_ref, kv_ref, out_ref, qs_ref, s_ref, m_ref, l_ref, o_ref):
    z, x, c = meta_ref[0], meta_ref[1], meta_ref[2]
    first, latest = first_ref[0] >> 9, first_ref[1]
    for block in range(8):
        to = (block % 2) * 64 + (block // 2) * 16
        for t in range(2):
            at = pl.ds(pl.multiple_of(c * 128 + t * 64 + (block % 4) * 16, 16), 16)
            for h in range(4):
                lanes = slice((h * 2 + t) * 128, (h * 2 + t + 1) * 128)
                qs_ref[to : to + 16, lanes] = q_ref[h * 2 + block // 4, at, :]
    factor = math.log2(math.e) / math.sqrt(DIM)
    m_ref[...] = jnp.full((8, 1024), FLOOR, F32)
    l_ref[...] = jnp.zeros((8, 1024), F32)
    o_ref[...] = jnp.zeros((128, 1024), F32)
    heads = [slice(h * 256, (h + 1) * 256) for h in range(4)]
    pairs = (z - first + 2) >> 1

    def tile(which, i):
        rows = slice(which * 64, which * 64 + 64)
        columns = []
        for j in (first + 2 * i, jnp.minimum(first + 2 * i + 1, 11)):
            columns.append(jnp.concatenate([kv_ref[0, j, rows, :], kv_ref[1, j, rows, :]], axis=0))
        return jnp.concatenate(columns, axis=1)

    def score(i, unused):
        j = first + 2 * i
        key = tile(0, i).astype(F32).T.astype(BF16)

        def note(s, lanes):
            s_ref[i, :, lanes] = s
            m_ref[:, lanes] = jnp.maximum(m_ref[:, lanes], jnp.max(s.reshape(32, 8, 256), axis=0))

        inside = (j * 512 >= latest) & (j + 1 < z)

        @pl.when(inside)
        def _():
            for lanes in heads:
                note(jnp.dot(key, qs_ref[:, lanes], preferred_element_type=F32) * factor, lanes)

        @pl.when(jnp.logical_not(inside))
        def _():
            row = lax.broadcasted_iota(jnp.int32, (256, 256), 0)
            place = j * 512 + (row >> 7) * 512 + x * 128 + (row & 127)
            query = z * 512 + c * 256 + lax.broadcasted_iota(jnp.int32, (256, 256), 1)
            allowed = (place >= start_ref[...]) & (place <= query)
            for lanes in heads:
                s = jnp.dot(key, qs_ref[:, lanes], preferred_element_type=F32) * factor
                note(jnp.where(allowed, s, NEG), lanes)

        return unused

    lax.fori_loop(0, pairs, score, 0)
    top = jnp.max(m_ref[...], axis=0, keepdims=True)

    def mix(i, unused):
        val = tile(1, i)
        for lanes in heads:
            p = jnp.exp2(s_ref[i, :, lanes] - top[:, lanes])
            l_ref[:, lanes] += jnp.sum(p.reshape(32, 8, 256), axis=0)
            o_ref[:, lanes] += jnp.dot(val, p.astype(BF16), preferred_element_type=F32)
        return unused

    lax.fori_loop(0, pairs, mix, 0)
    total = jnp.sum(l_ref[...], axis=0, keepdims=True)
    stats = [v.astype(F32) for v in split3(top) + split3(total)]
    stats = jnp.concatenate(stats + [jnp.zeros((2, 1024), F32)], axis=0)
    for h, lanes in enumerate(heads):
        for block in range(8):
            at = (block % 2) * 64 + (block // 2) * 16
            out_ref[h, block * 16 : block * 16 + 16, :] = o_ref[at : at + 16, lanes].astype(BF16)
        out_ref[h, 128:136, :] = stats[:, lanes].astype(BF16)


def combine(in_ref, out_ref):
    tops, totals = [], []
    for j in range(4):
        st = in_ref[j, 128:136, :].astype(F32)
        tops.append(st[0:1] + st[1:2] + st[2:3])
        totals.append(st[3:4] + st[4:5] + st[5:6])
    top = jnp.maximum(jnp.maximum(tops[0], tops[1]), jnp.maximum(tops[2], tops[3]))
    shares = [jnp.exp2(t - top) for t in tops]
    total = sum(w * t for w, t in zip(shares, totals))
    mixed = sum(in_ref[j, 0:128, :].astype(F32) * (shares[j] / total) for j in range(4))
    mixed = mixed.astype(BF16)
    for j in range(4):
        out_ref[j] = mixed


def output_project(meta_ref, own_ref, other_ref, a_ref, out_ref, o_ref):
    x, c = meta_ref[1], meta_ref[2]
    for step in range(4):
        at = away(x, -step) * 128
        o_ref[rows_of(at + c * 64, 64), :] = own_ref[step]
        o_ref[rows_of(at + 64 - c * 64, 64), :] = other_ref[step]
    dims = (((0,), (0,)), ((), ()))
    r = lax.dot_general(o_ref[...], a_ref[...].reshape(512, 256), dims, preferred_element_type=F32)
    out_ref[...] = r.astype(BF16).reshape(16, 64, 256)


def sum_output(in_ref, out_ref):
    for half in range(2):
        total = in_ref[half].astype(F32)
        for j in range(1, 8):
            total = total + in_ref[j * 2 + half].astype(F32)
        out_ref[:, half * 256 : (half + 1) * 256] = total.astype(BF16)


def trade(block, axis):
    return lax.all_to_all(block, axis, split_axis=0, concat_axis=0, tiled=True)


def gather(block, axis):
    return lax.all_gather(block, axis, axis=0, tiled=False)


def send(block, step):
    if step == 0:
        return block
    return lax.ppermute(block, "x", [(i, (i + step) % 4) for i in range(4)])


def partner(block):
    return lax.ppermute(block, "c", [(0, 1), (1, 0)])


def layer(tokens, query_weight, key_weight, value_weight, output_weight, segments):
    z, x, c = lax.axis_index("z"), lax.axis_index("x"), lax.axis_index("c")
    place = lax.iota(jnp.int32, 4)
    meta = jnp.where(place == 0, z, jnp.where(place == 1, x, c))
    starts, first = pl.pallas_call(
        find_starts,
        out_shape=[shape(1, 256, dtype=jnp.int32), shape(2, dtype=jnp.int32)],
        in_specs=[pl.BlockSpec(memory_space=s) for s in (pltpu.SMEM, pltpu.VMEM)],
        out_specs=[pl.BlockSpec(memory_space=s) for s in (pltpu.VMEM, pltpu.SMEM)],
        scratch_shapes=[],
        compiler_params=pltpu.CompilerParams(vmem_limit_bytes=4 << 20),
    )(meta, segments.reshape(24, 256))
    copies = pl.pallas_call(
        spread_tokens,
        out_shape=shape(8, 64, 512),
        in_specs=[pl.BlockSpec(memory_space=pl.ANY)],
        out_specs=pl.BlockSpec(memory_space=pl.ANY),
        scratch_shapes=[pltpu.SemaphoreType.DMA((8,))],
        compiler_params=pltpu.CompilerParams(vmem_limit_bytes=4 << 20),
    )(tokens.T)
    own = trade(copies, "y").reshape(512, 512)
    packed = call(
        pack_weights, [shape(160, 1024)] * 4,
        meta, query_weight, key_weight, value_weight, output_weight, smem=(0,),
    )
    weights = [send(packed[i], i) for i in range(4)]
    other = partner(own)
    partial, o_own = call(
        project, [shape(4, 384, 128), shape(4, 64, 1024)],
        meta, *weights, own, other, smem=(0,), limit=12,
        scratch=[
            pltpu.VMEM((1024, 512), BF16),
            pltpu.VMEM((384, 1024), BF16),
            pltpu.VMEM((384, 512), BF16),
        ],
    )
    o_other = partner(o_own)
    queries, spread = call(
        sum_projection,
        [shape(256, 128), shape(12, 128, 128)],
        trade(partial, "x"),
    )
    memory = trade(spread, "z")
    queries = gather(queries, ("x", "c"))
    memory = gather(memory, "c")
    mixed = call(
        attend, shape(4, 136, 256), meta, first, starts, queries, memory,
        smem=(0, 1),
        limit=16,
        scratch=[
            pltpu.VMEM((128, 1024), BF16),
            pltpu.VMEM((6, 256, 1024), F32),
            pltpu.VMEM((8, 1024), F32),
            pltpu.VMEM((8, 1024), F32),
            pltpu.VMEM((128, 1024), F32),
        ],
    )
    attended = trade(call(combine, shape(4, 128, 256), trade(mixed, "x")), "x")
    result = call(
        output_project, shape(16, 64, 256), meta, o_own, o_other, attended, smem=(0,), limit=12,
        scratch=[pltpu.VMEM((512, 1024), BF16)],
    )
    final = call(sum_output, shape(64, 512), trade(result, ("y", "c")))
    return final.T


def solution(mesh):
    grid = Mesh(mesh.devices.reshape(12, 8, 4, 2), ("z", "y", "x", "c"))
    head = ("y", "x", "c")
    placed = (P("z", head), P(head, None), P(head, None), P(head, None), P(head, None), P())
    return jax.shard_map(layer, mesh=grid, in_specs=placed, out_specs=P("z", head), check_vma=False)
```

```python
import math

import jax
import jax.numpy as jnp
from jax import lax
from jax.experimental import pallas as pl
from jax.experimental.pallas import tpu as pltpu
from jax.sharding import Mesh, PartitionSpec as P


DIM = 128
F32 = jnp.float32
BF16 = jnp.bfloat16
NEG = -1e30
FLOOR = -1e28


def call(body, outs, *args, smem=(), scratch=(), limit=8):
    specs = [
        pl.BlockSpec(memory_space=pltpu.SMEM if i in smem else pltpu.VMEM)
        for i in range(len(args))
    ]
    single = not isinstance(outs, (list, tuple))
    many = [outs] if single else list(outs)
    out = pl.pallas_call(
        body,
        out_shape=many,
        in_specs=specs,
        out_specs=[pl.BlockSpec(memory_space=pltpu.VMEM)] * len(many),
        scratch_shapes=list(scratch),
        compiler_params=pltpu.CompilerParams(vmem_limit_bytes=limit << 20),
    )(*args)
    return out[0] if single else out


def shape(*dims, dtype=BF16):
    return jax.ShapeDtypeStruct(dims, dtype)


def find_starts(meta_ref, seg_ref, start_ref, first_ref):
    at = meta_ref[0] * 2 + meta_ref[2]
    window = seg_ref[pl.ds(at, 1), :]
    lane = lax.broadcasted_iota(jnp.int32, (1, 256), 1)
    head = jnp.min(window)
    begin = jnp.sum((seg_ref[...] < head).astype(jnp.int32))
    changed = (lane > 0) & (window != pltpu.roll(window, 1, 1))
    starts = jnp.where(changed, at * 256 + lane, begin)
    for bit in range(8):
        moved = pltpu.roll(starts, 1 << bit, 1)
        starts = jnp.maximum(starts, jnp.where(lane >= 1 << bit, moved, 0))
    start_ref[...] = starts
    first_ref[0] = begin
    first_ref[1] = jnp.max(starts)


def away(x, step):
    return (x + step) & 3


def pack_weights(meta_ref, q_ref, k_ref, v_ref, o_ref, *outs):
    for step, out_ref in enumerate(outs):
        x = away(meta_ref[1], step)
        for y in range(8):
            src = pl.ds(pl.multiple_of((y * 4 + x) * 128, 128), 128)
            dst = slice(y * 128, (y + 1) * 128)
            out_ref[0:64, dst] = q_ref[:, src]
            out_ref[64:80, dst] = k_ref[:, src]
            out_ref[80:96, dst] = v_ref[:, src]
            out_ref[96:160, dst] = o_ref[:, src]


def rows_of(start, size):
    return pl.ds(pl.multiple_of(start, size), size)


def project(meta_ref, w0, w1, w2, w3, own_ref, other_ref, out_ref, o_ref, x_ref, all_ref, y_ref):
    x, c = meta_ref[1], meta_ref[2]
    for y in range(8):
        x_ref[rows_of(y * 128 + c * 64, 64), :] = own_ref[y * 64 : (y + 1) * 64, :]
        x_ref[rows_of(y * 128 + 64 - c * 64, 64), :] = other_ref[y * 64 : (y + 1) * 64, :]
    for step, w in enumerate((w0, w1, w2, w3)):
        all_ref[pl.ds(pl.multiple_of(away(x, -step) * 96, 32), 96), :] = w[0:96, :]
        o_ref[step] = w[96:160, :]
    y_ref[...] = jnp.dot(all_ref[...], x_ref[...], preferred_element_type=F32).astype(BF16)
    for j in range(4):
        for t in range(4):
            lanes = slice(t * 128, (t + 1) * 128)
            out_ref[j, t * 64 : (t + 1) * 64, :] = y_ref[j * 96 : j * 96 + 64, lanes]
            at = 256 + j * 16
            out_ref[t, at : at + 16, :] = y_ref[j * 96 + 64 : j * 96 + 80, lanes]
            at = 320 + j * 16
            out_ref[t, at : at + 16, :] = y_ref[j * 96 + 80 : j * 96 + 96, lanes]


def sum_projection(in_ref, q_ref, kv_ref):
    total = in_ref[0].astype(F32)
    for j in range(1, 4):
        total = total + in_ref[j].astype(F32)
    total = total.astype(BF16)
    q_ref[...] = total[0:256]
    for j in range(12):
        kv_ref[j] = total[256:384]


def spread_tokens(in_ref, out_ref, sems):
    copies = [pltpu.make_async_copy(in_ref, out_ref.at[y], sems.at[y]) for y in range(8)]
    for copy in copies:
        copy.start()
    for copy in copies:
        copy.wait()


def split3(value):
    high = value.astype(BF16)
    rest = value - high.astype(F32)
    mid = rest.astype(BF16)
    low = (rest - mid.astype(F32)).astype(BF16)
    return high, mid, low


def attend(meta_ref, first_ref, start_ref, q_ref, kv_ref, out_ref, qs_ref, s_ref, m_ref, l_ref, o_ref):
    z, x, c = meta_ref[0], meta_ref[1], meta_ref[2]
    first, latest = first_ref[0] >> 9, first_ref[1]
    for block in range(8):
        to = (block % 2) * 64 + (block // 2) * 16
        for t in range(2):
            at = pl.ds(pl.multiple_of(c * 128 + t * 64 + (block % 4) * 16, 16), 16)
            for h in range(4):
                lanes = slice((h * 2 + t) * 128, (h * 2 + t + 1) * 128)
                qs_ref[to : to + 16, lanes] = q_ref[h * 2 + block // 4, at, :]
    factor = math.log2(math.e) / math.sqrt(DIM)
    m_ref[...] = jnp.full((8, 1024), FLOOR, F32)
    l_ref[...] = jnp.zeros((8, 1024), F32)
    o_ref[...] = jnp.zeros((128, 1024), F32)
    heads = [slice(h * 256, (h + 1) * 256) for h in range(4)]
    pairs = (z - first + 2) >> 1

    def tile(which, i):
        rows = slice(which * 64, which * 64 + 64)
        columns = []
        for j in (first + 2 * i, jnp.minimum(first + 2 * i + 1, 11)):
            columns.append(jnp.concatenate([kv_ref[0, j, rows, :], kv_ref[1, j, rows, :]], axis=0))
        return jnp.concatenate(columns, axis=1)

    def score(i, unused):
        j = first + 2 * i
        key = tile(0, i).T

        def note(s, lanes):
            s_ref[i, :, lanes] = s
            m_ref[:, lanes] = jnp.maximum(m_ref[:, lanes], jnp.max(s.reshape(32, 8, 256), axis=0))

        inside = (j * 512 >= latest) & (j + 1 < z)

        @pl.when(inside)
        def _():
            for lanes in heads:
                note(jnp.dot(key, qs_ref[:, lanes], preferred_element_type=F32) * factor, lanes)

        @pl.when(jnp.logical_not(inside))
        def _():
            row = lax.broadcasted_iota(jnp.int32, (256, 256), 0)
            place = j * 512 + (row >> 7) * 512 + x * 128 + (row & 127)
            query = z * 512 + c * 256 + lax.broadcasted_iota(jnp.int32, (256, 256), 1)
            allowed = (place >= start_ref[...]) & (place <= query)
            for lanes in heads:
                s = jnp.dot(key, qs_ref[:, lanes], preferred_element_type=F32) * factor
                note(jnp.where(allowed, s, NEG), lanes)

        return unused

    lax.fori_loop(0, pairs, score, 0)
    top = jnp.max(m_ref[...], axis=0, keepdims=True)

    def mix(i, unused):
        val = tile(1, i)
        for lanes in heads:
            p = jnp.exp2(s_ref[i, :, lanes] - top[:, lanes])
            l_ref[:, lanes] += jnp.sum(p.reshape(32, 8, 256), axis=0)
            o_ref[:, lanes] += jnp.dot(val, p.astype(BF16), preferred_element_type=F32)
        return unused

    lax.fori_loop(0, pairs, mix, 0)
    total = jnp.sum(l_ref[...], axis=0, keepdims=True)
    stats = [v.astype(F32) for v in split3(top) + split3(total)]
    stats = jnp.concatenate(stats + [jnp.zeros((2, 1024), F32)], axis=0)
    for h, lanes in enumerate(heads):
        for block in range(8):
            at = (block % 2) * 64 + (block // 2) * 16
            out_ref[h, block * 16 : block * 16 + 16, :] = o_ref[at : at + 16, lanes].astype(BF16)
        out_ref[h, 128:136, :] = stats[:, lanes].astype(BF16)


def combine(in_ref, out_ref):
    tops, totals = [], []
    for j in range(4):
        st = in_ref[j, 128:136, :].astype(F32)
        tops.append(st[0:1] + st[1:2] + st[2:3])
        totals.append(st[3:4] + st[4:5] + st[5:6])
    top = jnp.maximum(jnp.maximum(tops[0], tops[1]), jnp.maximum(tops[2], tops[3]))
    shares = [jnp.exp2(t - top) for t in tops]
    total = sum(w * t for w, t in zip(shares, totals))
    mixed = sum(in_ref[j, 0:128, :].astype(F32) * (shares[j] / total) for j in range(4))
    mixed = mixed.astype(BF16)
    for j in range(8):
        out_ref[j] = mixed


def turn_output_weight(meta_ref, own_ref, other_ref, out_ref, o_ref, turned_ref):
    x, c = meta_ref[1], meta_ref[2]
    for step in range(4):
        at = away(x, -step) * 128
        o_ref[rows_of(at + c * 64, 64), :] = own_ref[step]
        o_ref[rows_of(at + 64 - c * 64, 64), :] = other_ref[step]
    turned_ref[...] = o_ref[...].T
    for y in range(8):
        out_ref[y * 64 : (y + 1) * 64, :] = turned_ref[rows_of(y * 128 + c * 64, 64), :]


def output_project(o_ref, in_ref, out_ref, a_ref):
    for j in range(4):
        for half in range(2):
            lanes = slice(half * 256, (half + 1) * 256)
            a_ref[j * 128 : (j + 1) * 128, lanes] = in_ref[j * 2 + half]
    r = jnp.dot(o_ref[...], a_ref[...], preferred_element_type=F32)
    out_ref[...] = r.astype(BF16).reshape(8, 64, 512)


def sum_output(in_ref, out_ref):
    total = in_ref[0].astype(F32)
    for j in range(1, 8):
        total = total + in_ref[j].astype(F32)
    out_ref[...] = total.astype(BF16)


def trade(block, axis):
    return lax.all_to_all(block, axis, split_axis=0, concat_axis=0, tiled=True)


def gather(block, axis):
    return lax.all_gather(block, axis, axis=0, tiled=False)


def send(block, step):
    if step == 0:
        return block
    return lax.ppermute(block, "x", [(i, (i + step) % 4) for i in range(4)])


def partner(block):
    return lax.ppermute(block, "c", [(0, 1), (1, 0)])


def layer(tokens, query_weight, key_weight, value_weight, output_weight, segments):
    z, x, c = lax.axis_index("z"), lax.axis_index("x"), lax.axis_index("c")
    place = lax.iota(jnp.int32, 4)
    meta = jnp.where(place == 0, z, jnp.where(place == 1, x, c))
    starts, first = pl.pallas_call(
        find_starts,
        out_shape=[shape(1, 256, dtype=jnp.int32), shape(2, dtype=jnp.int32)],
        in_specs=[pl.BlockSpec(memory_space=s) for s in (pltpu.SMEM, pltpu.VMEM)],
        out_specs=[pl.BlockSpec(memory_space=s) for s in (pltpu.VMEM, pltpu.SMEM)],
        scratch_shapes=[],
        compiler_params=pltpu.CompilerParams(vmem_limit_bytes=4 << 20),
    )(meta, segments.reshape(24, 256))
    copies = pl.pallas_call(
        spread_tokens,
        out_shape=shape(8, 64, 512),
        in_specs=[pl.BlockSpec(memory_space=pltpu.HBM)],
        out_specs=pl.BlockSpec(memory_space=pltpu.HBM),
        scratch_shapes=[pltpu.SemaphoreType.DMA((8,))],
        compiler_params=pltpu.CompilerParams(vmem_limit_bytes=4 << 20),
    )(tokens.T)
    own = trade(copies, "y").reshape(512, 512)
    packed = call(
        pack_weights, [shape(160, 1024)] * 4,
        meta, query_weight, key_weight, value_weight, output_weight, smem=(0,),
    )
    weights = [send(packed[i], i) for i in range(4)]
    other = partner(own)
    partial, o_own = call(
        project, [shape(4, 384, 128), shape(4, 64, 1024)],
        meta, *weights, own, other, smem=(0,), limit=12,
        scratch=[
            pltpu.VMEM((1024, 512), BF16),
            pltpu.VMEM((384, 1024), BF16),
            pltpu.VMEM((384, 512), BF16),
        ],
    )
    o_other = partner(o_own)
    queries, spread = call(
        sum_projection,
        [shape(256, 128), shape(12, 128, 128)],
        trade(partial, "x"),
    )
    memory = trade(spread, "z")
    queries = gather(queries, ("x", "c"))
    memory = gather(memory, "c")
    mixed = call(
        attend, shape(4, 136, 256), meta, first, starts, queries, memory,
        smem=(0, 1),
        limit=16,
        scratch=[
            pltpu.VMEM((128, 1024), BF16),
            pltpu.VMEM((6, 256, 1024), F32),
            pltpu.VMEM((8, 1024), F32),
            pltpu.VMEM((8, 1024), F32),
            pltpu.VMEM((128, 1024), F32),
        ],
    )
    turned = call(
        turn_output_weight, shape(512, 512), meta, o_own, o_other, smem=(0,), limit=12,
        scratch=[pltpu.VMEM((512, 1024), BF16), pltpu.VMEM((1024, 512), BF16)],
    )
    attended = call(combine, shape(8, 128, 256), trade(mixed, "x"))
    attended = trade(attended, ("x", "c"))
    result = call(
        output_project, shape(8, 64, 512), turned, attended, limit=12,
        scratch=[pltpu.VMEM((512, 512), BF16)],
    )
    final = call(sum_output, shape(64, 512), trade(result, "y"))
    return final.T


def solution(mesh):
    grid = Mesh(mesh.devices.reshape(12, 8, 4, 2), ("z", "y", "x", "c"))
    head = ("y", "x", "c")
    placed = (P("z", head), P(head, None), P(head, None), P(head, None), P(head, None), P())
    return jax.shard_map(layer, mesh=grid, in_specs=placed, out_specs=P("z", head), check_vma=False)
```

```python
import math

import jax
import jax.numpy as jnp
from jax import lax
from jax.experimental import pallas as pl
from jax.experimental.pallas import tpu as pltpu
from jax.sharding import Mesh, PartitionSpec as P


DIM = 128
F32 = jnp.float32
BF16 = jnp.bfloat16
NEG = -1e30
FLOOR = -1e28


def call(body, outs, *args, smem=(), scratch=(), limit=8):
    specs = [
        pl.BlockSpec(memory_space=pltpu.SMEM if i in smem else pltpu.VMEM)
        for i in range(len(args))
    ]
    single = not isinstance(outs, (list, tuple))
    many = [outs] if single else list(outs)
    out = pl.pallas_call(
        body,
        out_shape=many,
        in_specs=specs,
        out_specs=[pl.BlockSpec(memory_space=pltpu.VMEM)] * len(many),
        scratch_shapes=list(scratch),
        compiler_params=pltpu.CompilerParams(vmem_limit_bytes=limit << 20),
    )(*args)
    return out[0] if single else out


def shape(*dims, dtype=BF16):
    return jax.ShapeDtypeStruct(dims, dtype)


def find_starts(meta_ref, seg_ref, start_ref, first_ref):
    at = meta_ref[0] * 2 + meta_ref[2]
    window = seg_ref[pl.ds(at, 1), :]
    lane = lax.broadcasted_iota(jnp.int32, (1, 256), 1)
    head = jnp.min(window)
    begin = jnp.sum((seg_ref[...] < head).astype(jnp.int32))
    changed = (lane > 0) & (window != pltpu.roll(window, 1, 1))
    starts = jnp.where(changed, at * 256 + lane, begin)
    for bit in range(8):
        moved = pltpu.roll(starts, 1 << bit, 1)
        starts = jnp.maximum(starts, jnp.where(lane >= 1 << bit, moved, 0))
    start_ref[...] = starts
    first_ref[0] = begin
    first_ref[1] = jnp.max(starts)


def away(x, step):
    return (x + step) & 3


def pack_weights(meta_ref, q_ref, k_ref, v_ref, o_ref, *outs):
    for step, out_ref in enumerate(outs):
        x = away(meta_ref[1], step)
        for y in range(8):
            src = pl.ds(pl.multiple_of((y * 4 + x) * 128, 128), 128)
            dst = slice(y * 128, (y + 1) * 128)
            out_ref[0:64, dst] = q_ref[:, src]
            out_ref[64:80, dst] = k_ref[:, src]
            out_ref[80:96, dst] = v_ref[:, src]
            out_ref[96:160, dst] = o_ref[:, src]


def rows_of(start, size):
    return pl.ds(pl.multiple_of(start, size), size)


def project(meta_ref, w0, w1, w2, w3, own_ref, other_ref, out_ref, o_ref, x_ref, all_ref, y_ref):
    x, c = meta_ref[1], meta_ref[2]
    for y in range(8):
        x_ref[rows_of(y * 128 + c * 64, 64), :] = own_ref[y * 64 : (y + 1) * 64, :]
        x_ref[rows_of(y * 128 + 64 - c * 64, 64), :] = other_ref[y * 64 : (y + 1) * 64, :]
    for step, w in enumerate((w0, w1, w2, w3)):
        all_ref[pl.ds(pl.multiple_of(away(x, -step) * 96, 32), 96), :] = w[0:96, :]
        o_ref[step] = w[96:160, :]
    y_ref[...] = jnp.dot(all_ref[...], x_ref[...], preferred_element_type=F32).astype(BF16)
    for j in range(4):
        for t in range(4):
            lanes = slice(t * 128, (t + 1) * 128)
            out_ref[j, t * 64 : (t + 1) * 64, :] = y_ref[j * 96 : j * 96 + 64, lanes]
            at = 256 + j * 16
            out_ref[t, at : at + 16, :] = y_ref[j * 96 + 64 : j * 96 + 80, lanes]
            at = 320 + j * 16
            out_ref[t, at : at + 16, :] = y_ref[j * 96 + 80 : j * 96 + 96, lanes]


def sum_projection(in_ref, q_ref, kv_ref):
    total = in_ref[0].astype(F32)
    for j in range(1, 4):
        total = total + in_ref[j].astype(F32)
    total = total.astype(BF16)
    q_ref[...] = total[0:256]
    for j in range(12):
        kv_ref[j] = total[256:384]


def spread_tokens(in_ref, out_ref, sems):
    copies = [pltpu.make_async_copy(in_ref, out_ref.at[y], sems.at[y]) for y in range(8)]
    for copy in copies:
        copy.start()
    for copy in copies:
        copy.wait()


def split3(value):
    high = value.astype(BF16)
    rest = value - high.astype(F32)
    mid = rest.astype(BF16)
    low = (rest - mid.astype(F32)).astype(BF16)
    return high, mid, low


def attend(meta_ref, first_ref, start_ref, q_ref, kv_ref, out_ref, qs_ref, s_ref, m_ref, l_ref, o_ref):
    z, x, c = meta_ref[0], meta_ref[1], meta_ref[2]
    first, latest = first_ref[0] >> 9, first_ref[1]
    for block in range(8):
        to = (block % 2) * 64 + (block // 2) * 16
        for t in range(2):
            at = pl.ds(pl.multiple_of(c * 128 + t * 64 + (block % 4) * 16, 16), 16)
            for h in range(4):
                lanes = slice((h * 2 + t) * 128, (h * 2 + t + 1) * 128)
                qs_ref[to : to + 16, lanes] = q_ref[h * 2 + block // 4, at, :]
    factor = math.log2(math.e) / math.sqrt(DIM)
    m_ref[...] = jnp.full((8, 1024), FLOOR, F32)
    l_ref[...] = jnp.zeros((8, 1024), F32)
    o_ref[...] = jnp.zeros((128, 1024), F32)
    heads = [slice(h * 256, (h + 1) * 256) for h in range(4)]
    groups = (z - first + 4) >> 2

    def tile(which, i):
        rows = slice(which * 64, which * 64 + 64)
        columns = []
        for j in [jnp.minimum(first + 4 * i + g, 11) for g in range(4)]:
            columns.append(jnp.concatenate([kv_ref[0, j, rows, :], kv_ref[1, j, rows, :]], axis=0))
        return jnp.concatenate(columns, axis=1)

    def score(i, unused):
        j = first + 4 * i
        key = tile(0, i).T

        def note(s, lanes):
            s_ref[i, :, lanes] = s
            m_ref[:, lanes] = jnp.maximum(m_ref[:, lanes], jnp.max(s.reshape(64, 8, 256), axis=0))

        inside = (j * 512 >= latest) & (j + 3 < z)

        @pl.when(inside)
        def _():
            for lanes in heads:
                note(jnp.dot(key, qs_ref[:, lanes], preferred_element_type=F32) * factor, lanes)

        @pl.when(jnp.logical_not(inside))
        def _():
            row = lax.broadcasted_iota(jnp.int32, (512, 256), 0)
            place = j * 512 + (row >> 7) * 512 + x * 128 + (row & 127)
            query = z * 512 + c * 256 + lax.broadcasted_iota(jnp.int32, (512, 256), 1)
            allowed = (place >= start_ref[...]) & (place <= query)
            for lanes in heads:
                s = jnp.dot(key, qs_ref[:, lanes], preferred_element_type=F32) * factor
                note(jnp.where(allowed, s, NEG), lanes)

        return unused

    lax.fori_loop(0, groups, score, 0)
    top = jnp.max(m_ref[...], axis=0, keepdims=True)

    def mix(i, unused):
        val = tile(1, i)
        for lanes in heads:
            p = jnp.exp2(s_ref[i, :, lanes] - top[:, lanes])
            l_ref[:, lanes] += jnp.sum(p.reshape(64, 8, 256), axis=0)
            o_ref[:, lanes] += jnp.dot(val, p.astype(BF16), preferred_element_type=F32)
        return unused

    lax.fori_loop(0, groups, mix, 0)
    total = jnp.sum(l_ref[...], axis=0, keepdims=True)
    stats = [v.astype(F32) for v in split3(top) + split3(total)]
    stats = jnp.concatenate(stats + [jnp.zeros((2, 1024), F32)], axis=0)
    for h, lanes in enumerate(heads):
        for block in range(8):
            at = (block % 2) * 64 + (block // 2) * 16
            out_ref[h, block * 16 : block * 16 + 16, :] = o_ref[at : at + 16, lanes].astype(BF16)
        out_ref[h, 128:136, :] = stats[:, lanes].astype(BF16)


def combine(in_ref, out_ref):
    tops, totals = [], []
    for j in range(4):
        st = in_ref[j, 128:136, :].astype(F32)
        tops.append(st[0:1] + st[1:2] + st[2:3])
        totals.append(st[3:4] + st[4:5] + st[5:6])
    top = jnp.maximum(jnp.maximum(tops[0], tops[1]), jnp.maximum(tops[2], tops[3]))
    shares = [jnp.exp2(t - top) for t in tops]
    total = sum(w * t for w, t in zip(shares, totals))
    mixed = sum(in_ref[j, 0:128, :].astype(F32) * (shares[j] / total) for j in range(4))
    mixed = mixed.astype(BF16)
    for j in range(4):
        out_ref[j] = mixed


def output_project(meta_ref, own_ref, other_ref, a_ref, out_ref, o_ref):
    x, c = meta_ref[1], meta_ref[2]
    for step in range(4):
        at = away(x, -step) * 128
        o_ref[rows_of(at + c * 64, 64), :] = own_ref[step]
        o_ref[rows_of(at + 64 - c * 64, 64), :] = other_ref[step]
    dims = (((0,), (0,)), ((), ()))
    r = lax.dot_general(o_ref[...], a_ref[...].reshape(512, 256), dims, preferred_element_type=F32)
    out_ref[...] = r.astype(BF16).reshape(16, 64, 256)


def sum_output(in_ref, out_ref):
    for half in range(2):
        total = in_ref[half].astype(F32)
        for j in range(1, 8):
            total = total + in_ref[j * 2 + half].astype(F32)
        out_ref[:, half * 256 : (half + 1) * 256] = total.astype(BF16)


def trade(block, axis):
    return lax.all_to_all(block, axis, split_axis=0, concat_axis=0, tiled=True)


def gather(block, axis):
    return lax.all_gather(block, axis, axis=0, tiled=False)


def send(block, step):
    if step == 0:
        return block
    return lax.ppermute(block, "x", [(i, (i + step) % 4) for i in range(4)])


def partner(block):
    return lax.ppermute(block, "c", [(0, 1), (1, 0)])


def layer(tokens, query_weight, key_weight, value_weight, output_weight, segments):
    z, x, c = lax.axis_index("z"), lax.axis_index("x"), lax.axis_index("c")
    place = lax.iota(jnp.int32, 4)
    meta = jnp.where(place == 0, z, jnp.where(place == 1, x, c))
    starts, first = pl.pallas_call(
        find_starts,
        out_shape=[shape(1, 256, dtype=jnp.int32), shape(2, dtype=jnp.int32)],
        in_specs=[pl.BlockSpec(memory_space=s) for s in (pltpu.SMEM, pltpu.VMEM)],
        out_specs=[pl.BlockSpec(memory_space=s) for s in (pltpu.VMEM, pltpu.SMEM)],
        scratch_shapes=[],
        compiler_params=pltpu.CompilerParams(vmem_limit_bytes=4 << 20),
    )(meta, segments.reshape(24, 256))
    copies = pl.pallas_call(
        spread_tokens,
        out_shape=shape(8, 64, 512),
        in_specs=[pl.BlockSpec(memory_space=pl.ANY)],
        out_specs=pl.BlockSpec(memory_space=pl.ANY),
        scratch_shapes=[pltpu.SemaphoreType.DMA((8,))],
        compiler_params=pltpu.CompilerParams(vmem_limit_bytes=4 << 20),
    )(tokens.T)
    own = trade(copies, "y").reshape(512, 512)
    packed = call(
        pack_weights, [shape(160, 1024)] * 4,
        meta, query_weight, key_weight, value_weight, output_weight, smem=(0,),
    )
    weights = [send(packed[i], i) for i in range(4)]
    other = partner(own)
    partial, o_own = call(
        project, [shape(4, 384, 128), shape(4, 64, 1024)],
        meta, *weights, own, other, smem=(0,), limit=12,
        scratch=[
            pltpu.VMEM((1024, 512), BF16),
            pltpu.VMEM((384, 1024), BF16),
            pltpu.VMEM((384, 512), BF16),
        ],
    )
    o_other = partner(o_own)
    queries, spread = call(
        sum_projection,
        [shape(256, 128), shape(12, 128, 128)],
        trade(partial, "x"),
    )
    memory = trade(spread, "z")
    queries = gather(queries, ("x", "c"))
    memory = gather(memory, "c")
    mixed = call(
        attend, shape(4, 136, 256), meta, first, starts, queries, memory,
        smem=(0, 1),
        limit=16,
        scratch=[
            pltpu.VMEM((128, 1024), BF16),
            pltpu.VMEM((3, 512, 1024), F32),
            pltpu.VMEM((8, 1024), F32),
            pltpu.VMEM((8, 1024), F32),
            pltpu.VMEM((128, 1024), F32),
        ],
    )
    attended = trade(call(combine, shape(4, 128, 256), trade(mixed, "x")), "x")
    result = call(
        output_project, shape(16, 64, 256), meta, o_own, o_other, attended, smem=(0,), limit=12,
        scratch=[pltpu.VMEM((512, 1024), BF16)],
    )
    final = call(sum_output, shape(64, 512), trade(result, ("y", "c")))
    return final.T


def solution(mesh):
    grid = Mesh(mesh.devices.reshape(12, 8, 4, 2), ("z", "y", "x", "c"))
    head = ("y", "x", "c")
    placed = (P("z", head), P(head, None), P(head, None), P(head, None), P(head, None), P())
    return jax.shard_map(layer, mesh=grid, in_specs=placed, out_specs=P("z", head), check_vma=False)
```

```python
import math

import jax
import jax.numpy as jnp
from jax import lax
from jax.experimental import pallas as pl
from jax.experimental.pallas import tpu as pltpu
from jax.sharding import Mesh, PartitionSpec as P


DIM = 128
F32 = jnp.float32
BF16 = jnp.bfloat16
NEG = -1e30
FLOOR = -1e28


def call(body, outs, *args, smem=(), scratch=(), limit=8):
    specs = [
        pl.BlockSpec(memory_space=pltpu.SMEM if i in smem else pltpu.VMEM)
        for i in range(len(args))
    ]
    single = not isinstance(outs, (list, tuple))
    many = [outs] if single else list(outs)
    out = pl.pallas_call(
        body,
        out_shape=many,
        in_specs=specs,
        out_specs=[pl.BlockSpec(memory_space=pltpu.VMEM)] * len(many),
        scratch_shapes=list(scratch),
        compiler_params=pltpu.CompilerParams(vmem_limit_bytes=limit << 20),
    )(*args)
    return out[0] if single else out


def shape(*dims, dtype=BF16):
    return jax.ShapeDtypeStruct(dims, dtype)


def find_starts(meta_ref, seg_ref, start_ref, first_ref):
    at = meta_ref[0] * 2 + meta_ref[2]
    window = jnp.concatenate([seg_ref[pl.ds(at * 2, 1), :], seg_ref[pl.ds(at * 2 + 1, 1), :]], axis=1)
    lane = lax.broadcasted_iota(jnp.int32, (1, 256), 1)
    begin = jnp.sum((seg_ref[...] < window[:, 0:1]).astype(jnp.int32))
    changed = (lane > 0) & (window != pltpu.roll(window, 1, 1))
    starts = jnp.where(changed, at * 256 + lane, begin)
    for bit in range(8):
        moved = pltpu.roll(starts, 1 << bit, 1)
        starts = jnp.maximum(starts, jnp.where(lane >= 1 << bit, moved, 0))
    start_ref[...] = starts
    first_ref[0] = begin
    first_ref[1] = jnp.max(starts)


def away(x, step):
    return (x + step) & 3


def pack_weights(meta_ref, q_ref, k_ref, v_ref, o_ref, *outs):
    for step, out_ref in enumerate(outs):
        x = away(meta_ref[1], step)
        for y in range(8):
            src = pl.ds(pl.multiple_of((y * 4 + x) * 128, 128), 128)
            dst = slice(y * 128, (y + 1) * 128)
            out_ref[0:64, dst] = q_ref[:, src]
            out_ref[64:80, dst] = k_ref[:, src]
            out_ref[80:96, dst] = v_ref[:, src]
            out_ref[96:160, dst] = o_ref[:, src]


def rows_of(start, size):
    return pl.ds(pl.multiple_of(start, size), size)


def project(meta_ref, w0, w1, w2, w3, own_ref, other_ref, out_ref, o_ref, x_ref, all_ref, y_ref):
    x, c = meta_ref[1], meta_ref[2]
    for y in range(8):
        x_ref[rows_of(y * 128 + c * 64, 64), :] = own_ref[y * 64 : (y + 1) * 64, :]
        x_ref[rows_of(y * 128 + 64 - c * 64, 64), :] = other_ref[y * 64 : (y + 1) * 64, :]
    for step, w in enumerate((w0, w1, w2, w3)):
        all_ref[pl.ds(pl.multiple_of(away(x, -step) * 96, 32), 96), :] = w[0:96, :]
        o_ref[step] = w[96:160, :]
    y_ref[...] = jnp.dot(all_ref[...], x_ref[...], preferred_element_type=F32).astype(BF16)
    for j in range(4):
        for t in range(4):
            lanes = slice(t * 128, (t + 1) * 128)
            out_ref[j, t * 64 : (t + 1) * 64, :] = y_ref[j * 96 : j * 96 + 64, lanes]
            at = 256 + j * 16
            out_ref[t, at : at + 16, :] = y_ref[j * 96 + 64 : j * 96 + 80, lanes]
            at = 320 + j * 16
            out_ref[t, at : at + 16, :] = y_ref[j * 96 + 80 : j * 96 + 96, lanes]


def sum_projection(in_ref, q_ref, kv_ref):
    total = in_ref[0].astype(F32)
    for j in range(1, 4):
        total = total + in_ref[j].astype(F32)
    total = total.astype(BF16)
    q_ref[...] = total[0:256]
    for j in range(12):
        kv_ref[j] = total[256:384]


def spread_tokens(in_ref, out_ref, sems):
    copies = [pltpu.make_async_copy(in_ref, out_ref.at[y], sems.at[y]) for y in range(8)]
    for copy in copies:
        copy.start()
    for copy in copies:
        copy.wait()


def split3(value):
    high = value.astype(BF16)
    rest = value - high.astype(F32)
    mid = rest.astype(BF16)
    low = (rest - mid.astype(F32)).astype(BF16)
    return high, mid, low


def attend(meta_ref, first_ref, start_ref, q_ref, kv_ref, out_ref, qs_ref, s_ref, m_ref, l_ref, o_ref):
    z, x, c = meta_ref[0], meta_ref[1], meta_ref[2]
    first, latest = first_ref[0] >> 9, first_ref[1]
    for block in range(8):
        to = (block % 2) * 64 + (block // 2) * 16
        for t in range(2):
            at = pl.ds(pl.multiple_of(c * 128 + t * 64 + (block % 4) * 16, 16), 16)
            for h in range(4):
                lanes = slice((h * 2 + t) * 128, (h * 2 + t + 1) * 128)
                qs_ref[to : to + 16, lanes] = q_ref[h * 2 + block // 4, at, :]
    factor = math.log2(math.e) / math.sqrt(DIM)
    m_ref[...] = jnp.full((8, 1024), FLOOR, F32)
    l_ref[...] = jnp.zeros((8, 1024), F32)
    o_ref[...] = jnp.zeros((128, 1024), F32)
    heads = [slice(h * 256, (h + 1) * 256) for h in range(4)]
    groups = (z - first + 4) >> 2

    def tile(which, i):
        rows = slice(which * 64, which * 64 + 64)
        columns = []
        for j in [jnp.minimum(first + 4 * i + g, 11) for g in range(4)]:
            columns.append(jnp.concatenate([kv_ref[0, j, rows, :], kv_ref[1, j, rows, :]], axis=0))
        return jnp.concatenate(columns, axis=1)

    def score(i, unused):
        j = first + 4 * i
        key = tile(0, i).T

        def note(s, lanes):
            s_ref[i, :, lanes] = s
            m_ref[:, lanes] = jnp.maximum(m_ref[:, lanes], jnp.max(s.reshape(64, 8, 256), axis=0))

        inside = (j * 512 >= latest) & (j + 3 < z)

        @pl.when(inside)
        def _():
            for lanes in heads:
                note(jnp.dot(key, qs_ref[:, lanes], preferred_element_type=F32) * factor, lanes)

        @pl.when(jnp.logical_not(inside))
        def _():
            row = lax.broadcasted_iota(jnp.int32, (512, 256), 0)
            place = j * 512 + (row >> 7) * 512 + x * 128 + (row & 127)
            query = z * 512 + c * 256 + lax.broadcasted_iota(jnp.int32, (512, 256), 1)
            allowed = (place >= start_ref[...]) & (place <= query)
            for lanes in heads:
                s = jnp.dot(key, qs_ref[:, lanes], preferred_element_type=F32) * factor
                note(jnp.where(allowed, s, NEG), lanes)

        return unused

    lax.fori_loop(0, groups, score, 0)
    top = jnp.max(m_ref[...], axis=0, keepdims=True)

    def mix(i, unused):
        val = tile(1, i)
        for lanes in heads:
            p = jnp.exp2(s_ref[i, :, lanes] - top[:, lanes])
            l_ref[:, lanes] += jnp.sum(p.reshape(64, 8, 256), axis=0)
            o_ref[:, lanes] += jnp.dot(val, p.astype(BF16), preferred_element_type=F32)
        return unused

    lax.fori_loop(0, groups, mix, 0)
    total = jnp.sum(l_ref[...], axis=0, keepdims=True)
    stats = [v.astype(F32) for v in split3(top) + split3(total)]
    stats = jnp.concatenate(stats + [jnp.zeros((2, 1024), F32)], axis=0)
    for h, lanes in enumerate(heads):
        for block in range(8):
            at = (block % 2) * 64 + (block // 2) * 16
            out_ref[h, block * 16 : block * 16 + 16, :] = o_ref[at : at + 16, lanes].astype(BF16)
        out_ref[h, 128:136, :] = stats[:, lanes].astype(BF16)


def combine(in_ref, out_ref):
    tops, totals = [], []
    for j in range(4):
        st = in_ref[j, 128:136, :].astype(F32)
        tops.append(st[0:1] + st[1:2] + st[2:3])
        totals.append(st[3:4] + st[4:5] + st[5:6])
    top = jnp.maximum(jnp.maximum(tops[0], tops[1]), jnp.maximum(tops[2], tops[3]))
    shares = [jnp.exp2(t - top) for t in tops]
    total = sum(w * t for w, t in zip(shares, totals))
    mixed = sum(in_ref[j, 0:128, :].astype(F32) * (shares[j] / total) for j in range(4))
    mixed = mixed.astype(BF16)
    for j in range(4):
        out_ref[j] = mixed


def output_project(meta_ref, own_ref, other_ref, a_ref, out_ref, o_ref):
    x, c = meta_ref[1], meta_ref[2]
    for step in range(4):
        at = away(x, -step) * 128
        o_ref[rows_of(at + c * 64, 64), :] = own_ref[step]
        o_ref[rows_of(at + 64 - c * 64, 64), :] = other_ref[step]
    dims = (((0,), (0,)), ((), ()))
    r = lax.dot_general(o_ref[...], a_ref[...].reshape(512, 256), dims, preferred_element_type=F32)
    out_ref[...] = r.astype(BF16).reshape(16, 64, 256)


def sum_output(in_ref, out_ref):
    for half in range(2):
        total = in_ref[half].astype(F32)
        for j in range(1, 8):
            total = total + in_ref[j * 2 + half].astype(F32)
        out_ref[:, half * 256 : (half + 1) * 256] = total.astype(BF16)


def trade(block, axis):
    return lax.all_to_all(block, axis, split_axis=0, concat_axis=0, tiled=True)


def gather(block, axis):
    return lax.all_gather(block, axis, axis=0, tiled=False)


def send(block, step):
    if step == 0:
        return block
    return lax.ppermute(block, "x", [(i, (i + step) % 4) for i in range(4)])


def partner(block):
    return lax.ppermute(block, "c", [(0, 1), (1, 0)])


def layer(tokens, query_weight, key_weight, value_weight, output_weight, segments):
    z, x, c = lax.axis_index("z"), lax.axis_index("x"), lax.axis_index("c")
    place = lax.iota(jnp.int32, 4)
    meta = jnp.where(place == 0, z, jnp.where(place == 1, x, c))
    starts, first = pl.pallas_call(
        find_starts,
        out_shape=[shape(1, 256, dtype=jnp.int32), shape(2, dtype=jnp.int32)],
        in_specs=[pl.BlockSpec(memory_space=s) for s in (pltpu.SMEM, pltpu.VMEM)],
        out_specs=[pl.BlockSpec(memory_space=s) for s in (pltpu.VMEM, pltpu.SMEM)],
        scratch_shapes=[],
        compiler_params=pltpu.CompilerParams(vmem_limit_bytes=4 << 20),
    )(meta, segments.reshape(48, 128))
    copies = pl.pallas_call(
        spread_tokens,
        out_shape=shape(8, 64, 512),
        in_specs=[pl.BlockSpec(memory_space=pltpu.HBM)],
        out_specs=pl.BlockSpec(memory_space=pltpu.HBM),
        scratch_shapes=[pltpu.SemaphoreType.DMA((8,))],
        compiler_params=pltpu.CompilerParams(vmem_limit_bytes=4 << 20),
    )(pltpu.with_memory_space_constraint(tokens.T, pltpu.HBM))
    own = trade(copies, "y").reshape(512, 512)
    packed = call(
        pack_weights, [shape(160, 1024)] * 4,
        meta, query_weight, key_weight, value_weight, output_weight, smem=(0,),
    )
    weights = [send(packed[i], i) for i in range(4)]
    other = partner(own)
    partial, o_own = call(
        project, [shape(4, 384, 128), shape(4, 64, 1024)],
        meta, *weights, own, other, smem=(0,), limit=12,
        scratch=[
            pltpu.VMEM((1024, 512), BF16),
            pltpu.VMEM((384, 1024), BF16),
            pltpu.VMEM((384, 512), BF16),
        ],
    )
    o_other = partner(o_own)
    queries, spread = call(
        sum_projection,
        [shape(256, 128), shape(12, 128, 128)],
        trade(partial, "x"),
    )
    memory = trade(spread, "z")
    queries = gather(queries, ("x", "c"))
    memory = gather(memory, "c")
    mixed = call(
        attend, shape(4, 136, 256), meta, first, starts, queries, memory,
        smem=(0, 1),
        limit=16,
        scratch=[
            pltpu.VMEM((128, 1024), BF16),
            pltpu.VMEM((3, 512, 1024), F32),
            pltpu.VMEM((8, 1024), F32),
            pltpu.VMEM((8, 1024), F32),
            pltpu.VMEM((128, 1024), F32),
        ],
    )
    attended = trade(call(combine, shape(4, 128, 256), trade(mixed, "x")), "x")
    result = call(
        output_project, shape(16, 64, 256), meta, o_own, o_other, attended, smem=(0,), limit=12,
        scratch=[pltpu.VMEM((512, 1024), BF16)],
    )
    final = call(sum_output, shape(64, 512), trade(result, ("y", "c")))
    return final.T


def solution(mesh):
    grid = Mesh(mesh.devices.reshape(12, 8, 4, 2), ("z", "y", "x", "c"))
    head = ("y", "x", "c")
    placed = (P("z", head), P(head, None), P(head, None), P(head, None), P(head, None), P())
    return jax.shard_map(layer, mesh=grid, in_specs=placed, out_specs=P("z", head), check_vma=False)
```

```python
import math

import jax
import jax.numpy as jnp
from jax import lax
from jax.experimental import pallas as pl
from jax.experimental.pallas import tpu as pltpu
from jax.sharding import Mesh, PartitionSpec as P


DIM = 128
F32 = jnp.float32
BF16 = jnp.bfloat16
NEG = -1e30
FLOOR = -1e28


def call(body, outs, *args, smem=(), scratch=(), limit=8):
    specs = [
        pl.BlockSpec(memory_space=pltpu.SMEM if i in smem else pltpu.VMEM)
        for i in range(len(args))
    ]
    single = not isinstance(outs, (list, tuple))
    many = [outs] if single else list(outs)
    out = pl.pallas_call(
        body,
        out_shape=many,
        in_specs=specs,
        out_specs=[pl.BlockSpec(memory_space=pltpu.VMEM)] * len(many),
        scratch_shapes=list(scratch),
        compiler_params=pltpu.CompilerParams(vmem_limit_bytes=limit << 20),
    )(*args)
    return out[0] if single else out


def shape(*dims, dtype=BF16):
    return jax.ShapeDtypeStruct(dims, dtype)


def find_starts(meta_ref, seg_ref, start_ref, first_ref):
    at = meta_ref[0] * 2 + meta_ref[2]
    window = jnp.concatenate([seg_ref[pl.ds(at * 2, 1), :], seg_ref[pl.ds(at * 2 + 1, 1), :]], axis=1)
    lane = lax.broadcasted_iota(jnp.int32, (1, 256), 1)
    begin = jnp.sum((seg_ref[...] < window[:, 0:1]).astype(jnp.int32))
    changed = (lane > 0) & (window != pltpu.roll(window, 1, 1))
    starts = jnp.where(changed, at * 256 + lane, begin)
    for bit in range(8):
        moved = pltpu.roll(starts, 1 << bit, 1)
        starts = jnp.maximum(starts, jnp.where(lane >= 1 << bit, moved, 0))
    start_ref[...] = starts
    first_ref[0] = begin
    first_ref[1] = jnp.max(starts)


def away(x, step):
    return (x + step) & 3


def pack_weights(meta_ref, q_ref, k_ref, v_ref, o_ref, *outs):
    for step, out_ref in enumerate(outs):
        x = away(meta_ref[1], step)
        for y in range(8):
            src = pl.ds(pl.multiple_of((y * 4 + x) * 128, 128), 128)
            dst = slice(y * 128, (y + 1) * 128)
            out_ref[0:64, dst] = q_ref[:, src]
            out_ref[64:80, dst] = k_ref[:, src]
            out_ref[80:96, dst] = v_ref[:, src]
            out_ref[96:160, dst] = o_ref[:, src]


def rows_of(start, size):
    return pl.ds(pl.multiple_of(start, size), size)


def project(meta_ref, w0, w1, w2, w3, own_ref, other_ref, out_ref, o_ref, x_ref, all_ref, y_ref):
    x, c = meta_ref[1], meta_ref[2]
    for y in range(8):
        x_ref[rows_of(y * 128 + c * 64, 64), :] = own_ref[y * 64 : (y + 1) * 64, :]
        x_ref[rows_of(y * 128 + 64 - c * 64, 64), :] = other_ref[y * 64 : (y + 1) * 64, :]
    for step, w in enumerate((w0, w1, w2, w3)):
        all_ref[pl.ds(pl.multiple_of(away(x, -step) * 96, 32), 96), :] = w[0:96, :]
        o_ref[step] = w[96:160, :]
    y_ref[...] = jnp.dot(all_ref[...], x_ref[...], preferred_element_type=F32).astype(BF16)
    for j in range(4):
        for t in range(4):
            lanes = slice(t * 128, (t + 1) * 128)
            out_ref[j, t * 64 : (t + 1) * 64, :] = y_ref[j * 96 : j * 96 + 64, lanes]
            at = 256 + j * 16
            out_ref[t, at : at + 16, :] = y_ref[j * 96 + 64 : j * 96 + 80, lanes]
            at = 320 + j * 16
            out_ref[t, at : at + 16, :] = y_ref[j * 96 + 80 : j * 96 + 96, lanes]


def sum_projection(in_ref, q_ref, kv_ref):
    total = in_ref[0].astype(F32)
    for j in range(1, 4):
        total = total + in_ref[j].astype(F32)
    total = total.astype(BF16)
    q_ref[...] = total[0:256]
    for j in range(12):
        kv_ref[j] = total[256:384]


def spread_tokens(in_ref, out_ref, held_ref, sems):
    load = pltpu.make_async_copy(in_ref, held_ref, sems.at[8])
    load.start()
    load.wait()
    copies = [pltpu.make_async_copy(held_ref, out_ref.at[y], sems.at[y]) for y in range(8)]
    for copy in copies:
        copy.start()
    for copy in copies:
        copy.wait()


def split3(value):
    high = value.astype(BF16)
    rest = value - high.astype(F32)
    mid = rest.astype(BF16)
    low = (rest - mid.astype(F32)).astype(BF16)
    return high, mid, low


def attend(meta_ref, first_ref, start_ref, q_ref, kv_ref, out_ref, qs_ref, s_ref, m_ref, l_ref, o_ref):
    z, x, c = meta_ref[0], meta_ref[1], meta_ref[2]
    first, latest = first_ref[0] >> 9, first_ref[1]
    for block in range(8):
        to = (block % 2) * 64 + (block // 2) * 16
        for t in range(2):
            at = pl.ds(pl.multiple_of(c * 128 + t * 64 + (block % 4) * 16, 16), 16)
            for h in range(4):
                lanes = slice((h * 2 + t) * 128, (h * 2 + t + 1) * 128)
                qs_ref[to : to + 16, lanes] = q_ref[h * 2 + block // 4, at, :]
    factor = math.log2(math.e) / math.sqrt(DIM)
    m_ref[...] = jnp.full((8, 1024), FLOOR, F32)
    l_ref[...] = jnp.zeros((8, 1024), F32)
    o_ref[...] = jnp.zeros((128, 1024), F32)
    heads = [slice(h * 256, (h + 1) * 256) for h in range(4)]
    groups = (z - first + 4) >> 2

    def tile(which, i):
        rows = slice(which * 64, which * 64 + 64)
        columns = []
        for j in [jnp.minimum(first + 4 * i + g, 11) for g in range(4)]:
            columns.append(jnp.concatenate([kv_ref[0, j, rows, :], kv_ref[1, j, rows, :]], axis=0))
        return jnp.concatenate(columns, axis=1)

    def score(i, unused):
        j = first + 4 * i
        key = tile(0, i).T

        def note(s, lanes):
            s_ref[i, :, lanes] = s
            m_ref[:, lanes] = jnp.maximum(m_ref[:, lanes], jnp.max(s.reshape(64, 8, 256), axis=0))

        inside = (j * 512 >= latest) & (j + 3 < z)

        @pl.when(inside)
        def _():
            for lanes in heads:
                note(jnp.dot(key, qs_ref[:, lanes], preferred_element_type=F32) * factor, lanes)

        @pl.when(jnp.logical_not(inside))
        def _():
            row = lax.broadcasted_iota(jnp.int32, (512, 256), 0)
            place = j * 512 + (row >> 7) * 512 + x * 128 + (row & 127)
            query = z * 512 + c * 256 + lax.broadcasted_iota(jnp.int32, (512, 256), 1)
            allowed = (place >= start_ref[...]) & (place <= query)
            for lanes in heads:
                s = jnp.dot(key, qs_ref[:, lanes], preferred_element_type=F32) * factor
                note(jnp.where(allowed, s, NEG), lanes)

        return unused

    lax.fori_loop(0, groups, score, 0)
    top = jnp.max(m_ref[...], axis=0, keepdims=True)

    def mix(i, unused):
        val = tile(1, i)
        for lanes in heads:
            p = jnp.exp2(s_ref[i, :, lanes] - top[:, lanes])
            l_ref[:, lanes] += jnp.sum(p.reshape(64, 8, 256), axis=0)
            o_ref[:, lanes] += jnp.dot(val, p.astype(BF16), preferred_element_type=F32)
        return unused

    lax.fori_loop(0, groups, mix, 0)
    total = jnp.sum(l_ref[...], axis=0, keepdims=True)
    stats = [v.astype(F32) for v in split3(top) + split3(total)]
    stats = jnp.concatenate(stats + [jnp.zeros((2, 1024), F32)], axis=0)
    for h, lanes in enumerate(heads):
        for block in range(8):
            at = (block % 2) * 64 + (block // 2) * 16
            out_ref[h, block * 16 : block * 16 + 16, :] = o_ref[at : at + 16, lanes].astype(BF16)
        out_ref[h, 128:136, :] = stats[:, lanes].astype(BF16)


def combine(in_ref, out_ref):
    tops, totals = [], []
    for j in range(4):
        st = in_ref[j, 128:136, :].astype(F32)
        tops.append(st[0:1] + st[1:2] + st[2:3])
        totals.append(st[3:4] + st[4:5] + st[5:6])
    top = jnp.maximum(jnp.maximum(tops[0], tops[1]), jnp.maximum(tops[2], tops[3]))
    shares = [jnp.exp2(t - top) for t in tops]
    total = sum(w * t for w, t in zip(shares, totals))
    mixed = sum(in_ref[j, 0:128, :].astype(F32) * (shares[j] / total) for j in range(4))
    mixed = mixed.astype(BF16)
    for j in range(4):
        out_ref[j] = mixed


def output_project(meta_ref, own_ref, other_ref, a_ref, out_ref, o_ref):
    x, c = meta_ref[1], meta_ref[2]
    for step in range(4):
        at = away(x, -step) * 128
        o_ref[rows_of(at + c * 64, 64), :] = own_ref[step]
        o_ref[rows_of(at + 64 - c * 64, 64), :] = other_ref[step]
    dims = (((0,), (0,)), ((), ()))
    r = lax.dot_general(o_ref[...], a_ref[...].reshape(512, 256), dims, preferred_element_type=F32)
    out_ref[...] = r.astype(BF16).reshape(16, 64, 256)


def sum_output(in_ref, out_ref):
    for half in range(2):
        total = in_ref[half].astype(F32)
        for j in range(1, 8):
            total = total + in_ref[j * 2 + half].astype(F32)
        out_ref[:, half * 256 : (half + 1) * 256] = total.astype(BF16)


def trade(block, axis):
    return lax.all_to_all(block, axis, split_axis=0, concat_axis=0, tiled=True)


def gather(block, axis):
    return lax.all_gather(block, axis, axis=0, tiled=False)


def send(block, step):
    if step == 0:
        return block
    return lax.ppermute(block, "x", [(i, (i + step) % 4) for i in range(4)])


def partner(block):
    return lax.ppermute(block, "c", [(0, 1), (1, 0)])


def layer(tokens, query_weight, key_weight, value_weight, output_weight, segments):
    z, x, c = lax.axis_index("z"), lax.axis_index("x"), lax.axis_index("c")
    place = lax.iota(jnp.int32, 4)
    meta = jnp.where(place == 0, z, jnp.where(place == 1, x, c))
    starts, first = pl.pallas_call(
        find_starts,
        out_shape=[shape(1, 256, dtype=jnp.int32), shape(2, dtype=jnp.int32)],
        in_specs=[pl.BlockSpec(memory_space=s) for s in (pltpu.SMEM, pltpu.VMEM)],
        out_specs=[pl.BlockSpec(memory_space=s) for s in (pltpu.VMEM, pltpu.SMEM)],
        scratch_shapes=[],
        compiler_params=pltpu.CompilerParams(vmem_limit_bytes=4 << 20),
    )(meta, segments.reshape(48, 128))
    copies = pl.pallas_call(
        spread_tokens,
        out_shape=shape(8, 64, 512),
        in_specs=[pl.BlockSpec(memory_space=pltpu.HBM)],
        out_specs=pl.BlockSpec(memory_space=pltpu.HBM),
        scratch_shapes=[pltpu.VMEM((64, 512), BF16), pltpu.SemaphoreType.DMA((9,))],
        compiler_params=pltpu.CompilerParams(vmem_limit_bytes=4 << 20),
    )(pltpu.with_memory_space_constraint(tokens.T, pltpu.HBM))
    own = trade(copies, "y").reshape(512, 512)
    packed = call(
        pack_weights, [shape(160, 1024)] * 4,
        meta, query_weight, key_weight, value_weight, output_weight, smem=(0,),
    )
    weights = [send(packed[i], i) for i in range(4)]
    other = partner(own)
    partial, o_own = call(
        project, [shape(4, 384, 128), shape(4, 64, 1024)],
        meta, *weights, own, other, smem=(0,), limit=12,
        scratch=[
            pltpu.VMEM((1024, 512), BF16),
            pltpu.VMEM((384, 1024), BF16),
            pltpu.VMEM((384, 512), BF16),
        ],
    )
    o_other = partner(o_own)
    queries, spread = call(
        sum_projection,
        [shape(256, 128), shape(12, 128, 128)],
        trade(partial, "x"),
    )
    memory = trade(spread, "z")
    queries = gather(queries, ("x", "c"))
    memory = gather(memory, "c")
    mixed = call(
        attend, shape(4, 136, 256), meta, first, starts, queries, memory,
        smem=(0, 1),
        limit=16,
        scratch=[
            pltpu.VMEM((128, 1024), BF16),
            pltpu.VMEM((3, 512, 1024), F32),
            pltpu.VMEM((8, 1024), F32),
            pltpu.VMEM((8, 1024), F32),
            pltpu.VMEM((128, 1024), F32),
        ],
    )
    attended = trade(call(combine, shape(4, 128, 256), trade(mixed, "x")), "x")
    result = call(
        output_project, shape(16, 64, 256), meta, o_own, o_other, attended, smem=(0,), limit=12,
        scratch=[pltpu.VMEM((512, 1024), BF16)],
    )
    final = call(sum_output, shape(64, 512), trade(result, ("y", "c")))
    return final.T


def solution(mesh):
    grid = Mesh(mesh.devices.reshape(12, 8, 4, 2), ("z", "y", "x", "c"))
    head = ("y", "x", "c")
    placed = (P("z", head), P(head, None), P(head, None), P(head, None), P(head, None), P())
    return jax.shard_map(layer, mesh=grid, in_specs=placed, out_specs=P("z", head), check_vma=False)
```
